128 devices in a mesh: gz: 128 (over x, y, z, core).
Axes of the slice: x: 4, y: 4, z: 4, core: 2. Of those that a mesh axis runs over, the one named last changes fastest.
Arguments:
- moments: float32 [10, 1024, 128, 128], P(None, 'gz')
- shapes: float32 [1024, 3, 289], P('gz'), may hold values from -0.6 to 0.6
- anchors: int32 [1024, 3], P('gz'), may hold values from 0 to 1023, as said below
- synthesis: float32 [512, 289], replicated, may hold values from -6 to 6
- spreading: float32 [512, 2048], replicated, may hold values from 0 to 0.001953125
Outputs:
- moments_out: float32 [10, 1024, 128, 128], P(None, 'gz')
- shapes_out: float32 [1024, 3, 289], P('gz')
The draws below stay inside these ranges and needn't reach their ends.
Inputs may be any that keep to these rules, and one draw needn't show every extreme that they name: `anchors`: membrane m is owned by device m // 8; the slab of its box's first plane (anchor_z // 8) is its owner's, the one before or the one after, cyclically over 1024 planes. Rows and columns lie below 128.
All inputs are finite; a program needn't handle non-finite values.
Results may differ from the reference program's by a relative error of at most 0.00017.
Values sent between devices are 32-bit elements; how exact they have to be, the bound alone decides.
No kernel may reach another device: no remote copies, remote signals or barrier semaphores. Data moves between devices by JAX's collectives and lax.ppermute only.
A program may use at most 256 MiB of HBM per device.

```python
import jax
import jax.numpy as jnp
from jax import lax

PL = 8
NYX = 128
MEM_DEV = 8
LMAX = 16
NPTS = 512
BZ = 8
BXY = 16
STEPS = 3
NCOEF = 289
NZ = 1024
MEMBRANES = 1024


COMPONENT_PAIRS = ((0, 0), (1, 1), (2, 2), (0, 1), (0, 2), (1, 2))


def draw_moments(key, part):
    keys = jax.random.split(key, 3)
    grid = (NZ, NYX, NYX)
    density = 1.0 + 0.02 * jax.random.normal(keys[0], grid, jnp.float32)
    momentum = 0.04 * jax.random.normal(keys[1], (3,) + grid, jnp.float32)
    noise = 0.01 * jax.random.normal(keys[2], (6,) + grid, jnp.float32)
    seconds = []
    for position, (axis_a, axis_b) in enumerate(COMPONENT_PAIRS):
        current = momentum[axis_a] * momentum[axis_b] + noise[position]
        if axis_a == axis_b:
            current = current + density / 3.0
        seconds.append(current)
    return jnp.concatenate([density[None], momentum, jnp.stack(seconds)], axis=0)


def draw_anchors(key, part):
    keys = jax.random.split(key, 4)
    owners = jnp.arange(MEMBRANES, dtype=jnp.int32) // MEM_DEV
    drift = jax.random.randint(keys[0], (MEMBRANES,), -1, 2, dtype=jnp.int32)
    inside = jax.random.randint(keys[1], (MEMBRANES,), 0, PL, dtype=jnp.int32)
    plane_first = ((owners + drift) * PL + inside) % NZ
    plane_first = plane_first.at[MEMBRANES - 1].set(NZ - 1)
    row_first = jax.random.randint(keys[2], (MEMBRANES,), 0, NYX, dtype=jnp.int32)
    row_first = row_first.at[0].set(0)
    column_first = jax.random.randint(keys[3], (MEMBRANES,), 0, NYX, dtype=jnp.int32)
    return jnp.stack([plane_first, row_first, column_first], axis=1)


def block_levels(stream_key, shape, cuts, low, largest):
    level = 1.0
    for dim, shards_of in cuts:
        steps = jax.random.uniform(jax.random.fold_in(jax.random.fold_in(stream_key, 6), dim), (shards_of,), jnp.float32, low / len(cuts), largest / len(cuts))
        level = level * jnp.repeat(jnp.exp(steps), shape[dim] // shards_of).reshape((-1,) + (1,) * (len(shape) - 1 - dim))
    return level


def scatter_about(key, extent, scale, limit, shards=(), kind=jnp.bfloat16):
    values = scale * jax.random.normal(key, extent, jnp.float32)
    if shards:
        values = values * block_levels(key, extent, shards, -0.22, 0.18)
    return jnp.clip(values, -limit, limit).astype(kind)


def setup_inputs(seed: int = 0) -> dict:
    splits = jax.random.split(jax.random.key(seed), 6)
    return {
        "moments": draw_moments(jax.random.fold_in(splits[5], 71), 0),
        "shapes": scatter_about(splits[1], (MEMBRANES, 3, NCOEF), 0.1, 0.6, ((0, 128),), jnp.float32),
        "anchors": draw_anchors(jax.random.fold_in(splits[5], 71), 0),
        "synthesis": scatter_about(splits[3], (NPTS, NCOEF), 1.0, 6.0, (), jnp.float32),
        "spreading": jnp.clip(jax.random.uniform(splits[4], (NPTS, BZ * BXY * BXY), jnp.float32, 0.0, 0.001953125), 0.0, 0.001953125),
    }


RELAX_RATE = 1.25
STIFF_SCALE = 0.002
MOBILITY = 0.5
PRECISE = lax.Precision.HIGHEST
COMPONENT_PAIRS = ((0, 0), (1, 1), (2, 2), (0, 1), (0, 2), (1, 2))


def lattice_links():
    links = []
    for along_z in (-1, 0, 1):
        for along_y in (-1, 0, 1):
            for along_x in (-1, 0, 1):
                links.append((along_z, along_y, along_x))
    return links


def link_weight(link):
    length = abs(link[0]) + abs(link[1]) + abs(link[2])
    return (8.0 / 27.0, 2.0 / 27.0, 1.0 / 54.0, 1.0 / 216.0)[length]


def rebuild_table():
    table_rows = []
    for link in lattice_links():
        weight = link_weight(link)
        squared = link[0] * link[0] + link[1] * link[1] + link[2] * link[2]
        entries = [weight * (1.0 - 1.5 * (squared - 1.0))]
        entries += [3.0 * weight * link[axis_a] for axis_a in range(3)]
        for axis_a, axis_b in COMPONENT_PAIRS:
            if axis_a == axis_b:
                entries.append(4.5 * weight * (link[axis_a] * link[axis_a] - 1.0 / 3.0))
            else:
                entries.append(9.0 * weight * link[axis_a] * link[axis_b])
        table_rows.append(entries)
    return jnp.asarray(table_rows, dtype=jnp.float32)


def moment_table():
    links = lattice_links()
    table_rows = [[1.0 for link in links]]
    for axis_a in range(3):
        table_rows.append([float(link[axis_a]) for link in links])
    for axis_a, axis_b in COMPONENT_PAIRS:
        table_rows.append([float(link[axis_a] * link[axis_b]) for link in links])
    return jnp.asarray(table_rows, dtype=jnp.float32)


def degree_stiffness(coefficient_count):
    numbers = jnp.arange(coefficient_count, dtype=jnp.int32)
    degree = jnp.zeros((coefficient_count,), jnp.int32)
    for degree_step in range(1, LMAX + 1):
        degree = degree + (numbers >= degree_step * degree_step).astype(jnp.int32)
    return STIFF_SCALE * (degree * (degree + 1) + 2).astype(jnp.float32)


def collide(moments, force_field):
    density = moments[0]
    momentum = moments[1:4]
    velocity = momentum + 0.5 * force_field
    seconds = []
    for position, (axis_a, axis_b) in enumerate(COMPONENT_PAIRS):
        current = moments[4 + position]
        target = velocity[axis_a] * velocity[axis_b]
        if axis_a == axis_b:
            target = target + density / 3.0
        source = force_field[axis_a] * velocity[axis_b] + velocity[axis_a] * force_field[axis_b]
        seconds.append(current + RELAX_RATE * (target - current) + (1.0 - 0.5 * RELAX_RATE) * source)
    return jnp.concatenate([density[None], momentum + force_field, jnp.stack(seconds)], axis=0)


def stream_planes(extended, planes):
    distributions = jnp.einsum('qm,mzyx->qzyx', rebuild_table(), extended, precision=PRECISE)
    moved = []
    for q_index, link in enumerate(lattice_links()):
        source = distributions[q_index, 1 - link[0]:1 - link[0] + planes]
        moved.append(jnp.roll(source, (link[1], link[2]), axis=(1, 2)))
    return jnp.einsum('mq,qzyx->mzyx', moment_table(), jnp.stack(moved), precision=PRECISE)


def reference(moments, shapes, anchors, synthesis, spreading):
    total_planes = moments.shape[1]
    side_cells = moments.shape[2]
    block_count = total_planes // PL
    membranes = shapes.shape[0]
    stiffness = degree_stiffness(shapes.shape[2])
    box_depth = jnp.arange(BZ, dtype=jnp.int32)
    across = jnp.arange(BXY, dtype=jnp.int32)
    plane_ids = (anchors[:, 0:1] + box_depth[None, :]) % total_planes
    row_ids = (anchors[:, 1:2] + across[None, :]) % side_cells
    column_ids = (anchors[:, 2:3] + across[None, :]) % side_cells

    def add_box(force_sum, pieces):
        one_box, planes_at, rows_at, columns_at = pieces
        force_sum = force_sum.at[:, planes_at[:, None, None], rows_at[None, :, None], columns_at[None, None, :]].add(one_box)
        return force_sum, None

    for iteration in range(STEPS):
        coefs = -stiffness * shapes
        surface = jnp.einsum('mcn,pn->mcp', coefs, synthesis, precision=PRECISE)
        boxes = jnp.einsum('mcp,pq->mcq', surface, spreading, precision=PRECISE).reshape(membranes, 3, BZ, BXY, BXY)
        empty_field = jnp.zeros((3, total_planes, side_cells, side_cells), jnp.float32)
        force_field, unused = lax.scan(add_box, empty_field, (boxes, plane_ids, row_ids, column_ids))
        post = collide(moments, force_field)
        padded = jnp.concatenate([post[:, -1:], post, post[:, :1]], axis=1)

        def one_block(first_plane):
            return stream_planes(lax.dynamic_slice_in_dim(padded, first_plane, PL + 2, 1), PL)

        blocks = lax.map(one_block, jnp.arange(block_count, dtype=jnp.int32) * PL)
        moments = jnp.transpose(blocks, (1, 0, 2, 3, 4)).reshape(10, total_planes, side_cells, side_cells)
        velocity = moments[1:4]
        sampled = velocity[:, plane_ids[:, :, None, None], row_ids[:, None, :, None], column_ids[:, None, None, :]]
        sampled = jnp.transpose(sampled, (1, 0, 2, 3, 4)).reshape(membranes, 3, BZ * BXY * BXY)
        surface_speed = jnp.einsum('mcq,pq->mcp', sampled, spreading, precision=PRECISE)
        shapes = shapes + MOBILITY * jnp.einsum('mcp,pn->mcn', surface_speed, synthesis, precision=PRECISE)
    return moments, shapes
```

```python
import functools

import jax
import jax.numpy as jnp
from jax import lax
from jax.experimental import pallas as pl
from jax.experimental.pallas import tpu as pltpu
from jax.sharding import PartitionSpec as P

LMAX = 16
BZ = 8
BXY = 16
STEPS = 3
STIFF_SCALE = 0.002
MOBILITY = 0.5

PLANES = 8
SIDE = 128
OWNED = 8
COEFS = 289
LANES = 384
CELLS = 2048
POINTS = 512
GROUP = OWNED * 3
BLOCKS = 5
ROWS = GROUP * BLOCKS
ANCHOR_LANE = 300
FIELDS = 10
PADDED = 144
CHUNK = 16
JK = ((0, 0), (1, 0), (2, 0), (0, 1), (1, 1), (0, 2))

ANY = pl.BlockSpec(memory_space=pl.ANY)
VMEM = pl.BlockSpec(memory_space=pltpu.VMEM)
SMEM = pl.BlockSpec(memory_space=pltpu.SMEM)
F32 = jnp.float32
BF16 = jnp.bfloat16


def shifted(block, distance):
    devices = lax.axis_size("gz")
    return lax.ppermute(block, "gz", [((i - distance) % devices, i) for i in range(devices)])


def split(value):
    high = value.astype(BF16)
    return high, (value - high.astype(F32)).astype(BF16)


def place(group):
    return group // 5, (group % 5) * GROUP


def couple_kernel(synthesis_ref, spreading_ref, high_ref, low_ref):
    s_high, s_low = split(synthesis_ref[...])
    w_high, w_low = split(spreading_ref[...])
    dot = functools.partial(
        lax.dot_general, dimension_numbers=(((0,), (0,)), ((), ())), preferred_element_type=F32
    )
    total = dot(s_high, w_high) + (dot(s_high, w_low) + dot(s_low, w_high))
    high, low = split(total)
    high_ref[...] = high
    low_ref[...] = low


def couple(synthesis, spreading):
    width = 512
    shape = jax.ShapeDtypeStruct((LANES, CELLS), BF16)
    return pl.pallas_call(
        couple_kernel,
        out_shape=(shape, shape),
        grid=(CELLS // width,),
        in_specs=[
            pl.BlockSpec((POINTS, LANES), lambda i: (0, 0)),
            pl.BlockSpec((POINTS, width), lambda i: (0, i)),
        ],
        out_specs=[pl.BlockSpec((LANES, width), lambda i: (0, i))] * 2,
        cost_estimate=pl.CostEstimate(
            flops=6 * LANES * POINTS * CELLS, bytes_accessed=8 * 2**20, transcendentals=0
        ),
        name="couple",
    )(synthesis, spreading)


def pack_kernel(first_ref, last_ref, small_ref, up_ref, down_ref):
    for out_ref, plane_ref in ((up_ref, last_ref), (down_ref, first_ref)):
        out_ref[0:FIELDS] = plane_ref[:, 0]
        for part in range(3):
            block, row = place(part)
            out_ref[FIELDS + block, row : row + GROUP] = small_ref[:, part * 128 : part * 128 + 128]


def pack(moments, small):
    shape = jax.ShapeDtypeStruct((FIELDS + 1, SIDE, SIDE), F32)
    whole = pl.BlockSpec((FIELDS + 1, SIDE, SIDE), lambda i: (0, 0, 0))
    return pl.pallas_call(
        pack_kernel,
        out_shape=(shape, shape),
        grid=(1,),
        in_specs=[
            pl.BlockSpec((FIELDS, 1, SIDE, SIDE), lambda i: (0, 0, 0, 0)),
            pl.BlockSpec((FIELDS, 1, SIDE, SIDE), lambda i: (0, PLANES - 1, 0, 0)),
            pl.BlockSpec((GROUP, LANES), lambda i: (0, 0)),
        ],
        out_specs=[whole, whole],
        name="pack",
    )(moments, moments, small)


def spread_x(zero, one, two):
    plus = zero if two is None else zero + two
    minus = plus
    if one is not None:
        plus, minus = plus + one, plus - one
    plus = pltpu.roll(plus, 1, 1)
    minus = pltpu.roll(minus, SIDE - 1, 1)
    both = plus + minus
    return (4.0 * zero + both, plus - minus, both)


def collide_rows(m, force):
    unit = 1.0 / 216.0
    rho = m[0]
    u = [m[1 + a] + 0.5 * force[a] for a in range(3)]
    t = [0.625 * u[a] + 0.375 * force[a] for a in range(3)]
    v = [(9.0 * unit) * u[a] for a in range(3)]
    line = [(3.0 * unit) * (m[1 + a] + force[a]) for a in range(3)]
    shared = (0.375 * unit) * rho
    square = [shared - (1.125 * unit) * m[4 + a] + v[a] * t[a] for a in range(3)]
    cross = [
        v[a] * t[b] + v[b] * t[a] - (2.25 * unit) * m[7 + n]
        for n, (a, b) in enumerate(((0, 1), (0, 2), (1, 2)))
    ]
    cell = unit * rho - (1.0 / 3.0) * (square[0] + square[1] + square[2])
    return cell, line, square, cross


def step_kernel(first, last, *refs):
    refs = list(refs)
    slots_ref = refs.pop(0)
    high_ref, low_ref, moments_hbm, up_hbm, down_hbm = refs[:5]
    del refs[:5]
    if first:
        own_ref, below_ref, above_ref = refs[:3]
        del refs[:3]
    else:
        state_ref, sum_ref = refs[:2]
        del refs[:2]
    out_hbm, newsum_ref = refs[:2]
    del refs[:2]
    if not last:
        newstate_ref, sendup_hbm, senddown_hbm = refs[:3]
        del refs[:3]
    (
        old, new, velocity, force, boxes, sampled, tail_up, tail_down,
        shifts, stills, ring, middle, state,
        in_sem, halo_sem, out_sem, send_sem,
    ) = refs

    up_blocks = up_hbm.shape[0] - FIELDS
    down_blocks = down_hbm.shape[0] - FIELDS
    fetch_tails = [
        pltpu.make_async_copy(up_hbm.at[pl.ds(FIELDS, up_blocks)], tail_up.at[pl.ds(0, up_blocks)], halo_sem.at[0]),
        pltpu.make_async_copy(down_hbm.at[pl.ds(FIELDS, down_blocks)], tail_down.at[pl.ds(0, down_blocks)], halo_sem.at[1]),
    ]
    fetch_planes = [pltpu.make_async_copy(up_hbm.at[pl.ds(0, FIELDS)], old.at[:, 0], in_sem.at[0])]
    for z in range(PLANES):
        fetch_planes.append(
            pltpu.make_async_copy(moments_hbm.at[:, z], old.at[:, z + 1], in_sem.at[z + 1])
        )
    fetch_planes.append(
        pltpu.make_async_copy(down_hbm.at[pl.ds(0, FIELDS)], old.at[:, PLANES + 1], in_sem.at[PLANES + 1])
    )
    for copy in fetch_tails:
        copy.start()
    for copy in fetch_planes:
        copy.start()

    force[...] = jnp.zeros_like(force)
    sampled[...] = jnp.zeros_like(sampled)
    for copy in fetch_tails:
        copy.wait()

    for part in range(3):
        lanes = slice(part * 128, part * 128 + 128)

        def tail(ref, owner):
            block, row = place(owner * 3 + part)
            return ref[block, row : row + GROUP]

        for owner in range(BLOCKS):
            rows = slice(owner * GROUP, owner * GROUP + GROUP)
            if first:
                value = (
                    below_ref[:, lanes] if owner == 0
                    else tail(tail_up, 0) if owner == 1
                    else own_ref[:, lanes] if owner == 2
                    else tail(tail_down, 0) if owner == 3
                    else above_ref[:, lanes]
                )
                if part == 2:
                    lane = lax.broadcasted_iota(jnp.int32, value.shape, 1)
                    value = jnp.where(lane < COEFS - 256, value, 0.0)
            else:
                value = state_ref[rows, lanes]
                if owner < 3:
                    value = value + MOBILITY * tail(tail_up, owner)
                if owner > 0:
                    value = value + MOBILITY * tail(tail_down, owner - 1)
            state[rows, lanes] = value

    number = lax.broadcasted_iota(jnp.int32, (1, LANES), 1)
    degree = jnp.zeros((1, LANES), jnp.int32)
    for step in range(1, LMAX + 1):
        degree = degree + (number >= step * step).astype(jnp.int32)
    stiffness = STIFF_SCALE * (degree * (degree + 1) + 2).astype(F32)
    coef_high, coef_low = split(-stiffness * state[...])
    both = jnp.concatenate([coef_high, coef_low], axis=0)
    for part in range(CELLS // 512):
        lanes = slice(part * 512, part * 512 + 512)
        main = jnp.dot(both, high_ref[:, lanes], preferred_element_type=F32)
        rest = jnp.dot(coef_high, low_ref[:, lanes], preferred_element_type=F32)
        whole = main[:ROWS] + (main[ROWS:] + rest)
        for chunk in range(4):
            boxes[part * 4 + chunk] = whole[:, chunk * 128 : chunk * 128 + 128]

    lane = lax.broadcasted_iota(jnp.int32, (8, SIDE), 1)
    inside = lax.broadcasted_iota(jnp.int32, (8, SIDE), 0)
    row_bits = [(inside & (1 << bit)) != 0 for bit in range(3)]

    def place_box(slot, carry):
        above = slots_ref[slot * 3]
        row = slots_ref[slot * 3 + 1]
        column = slots_ref[slot * 3 + 2]

        @pl.when(jnp.logical_and(above >= -BZ, above <= PLANES))
        def _():
            here = ((lane - column) & (SIDE - 1)) < BXY

            def place_plane(k, carry):
                for c in range(3):
                    halves = []
                    for half in range(2):
                        cells = boxes[k * 2 + half, pl.ds(slot * 3 + c, 1)]
                        cells = jnp.broadcast_to(cells, (8, SIDE))
                        for bit in range(3):
                            turned = pltpu.roll(cells, SIDE - (BXY << bit), 1)
                            cells = jnp.where(row_bits[bit], turned, cells)
                        halves.append(jnp.where(here, pltpu.roll(cells, column, 1), 0.0))
                    where = (c, above + k + 1, pl.ds(row, BXY))
                    force[where] = force[where] + jnp.concatenate(halves, axis=0)
                return carry

            lax.fori_loop(
                jnp.maximum(0, -1 - above), jnp.minimum(BZ, PLANES + 1 - above), place_plane, 0
            )

        return carry

    lax.fori_loop(0, BLOCKS * OWNED, place_box, 0)

    def fold(z, carry):
        for c in range(3):
            force[c, z, 0:BXY] = force[c, z, 0:BXY] + force[c, z, SIDE:PADDED]
        return carry

    lax.fori_loop(0, PLANES + 2, fold, 0)

    def stream_plane(z, carry):
        pltpu.make_async_copy(moments_hbm.at[:, 0], old.at[:, z], in_sem.at[z]).wait()

        def collide_chunk(step, carry):
            y = pl.multiple_of(step * CHUNK, CHUNK)
            rows = pl.ds(y, CHUNK)
            m = [old[f, z, rows] for f in range(FIELDS)]
            cell, line, square, cross = collide_rows(m, [force[c, z, rows] for c in range(3)])
            even = [
                spread_x(cell, line[2], square[2]),
                spread_x(line[1], cross[2], None),
                spread_x(square[1], None, None),
            ]
            twice = spread_x(square[0], None, None)
            odd = [spread_x(line[0], cross[1], None), spread_x(cross[0], None, None)]
            moved = pl.ds(y + 8, CHUNK)
            for k in range(3):
                ends = even[0][k] + even[2][k]
                shifts[k, moved] = ends + even[1][k]
                shifts[3 + k, moved] = ends - even[1][k]
                shifts[6 + k, moved] = odd[0][k] + odd[1][k]
                shifts[9 + k, moved] = odd[0][k] - odd[1][k]
                shifts[12 + k, moved] = twice[k]
                stills[k, rows] = 4.0 * even[0][k]
                stills[3 + k, rows] = 4.0 * odd[0][k]
            return carry

        lax.fori_loop(0, SIDE // CHUNK, collide_chunk, 0)
        for field in range(15):
            shifts[field, 7:8] = shifts[field, SIDE + 7 : SIDE + 8]
            shifts[field, SIDE + 8 : SIDE + 9] = shifts[field, 8:9]
        parity = z % 2
        inner = jnp.clip(z - 2, 0, PLANES - 1)

        for step in range(SIDE // CHUNK):
            y = step * CHUNK
            rows = slice(y, y + CHUNK)
            after = slice(y + 7, y + 7 + CHUNK)
            before = slice(y + 9, y + 9 + CHUNK)
            even, odd, twice = {}, {}, {}
            for k in range(3):
                for target, plus, minus, still in (
                    (even, k, 3 + k, lambda k=k: stills[k, rows]),
                    (odd, 6 + k, 9 + k, lambda k=k: stills[3 + k, rows]),
                    (twice, 12 + k, 12 + k, lambda k=k: 4.0 * shifts[12 + k, y + 8 : y + 8 + CHUNK]),
                ):
                    up, down = shifts[plus, after], shifts[minus, before]
                    both = up + down
                    target[0, k] = still() + both
                    if k < 2:
                        target[1, k] = up - down
                    if k < 1:
                        target[2, k] = both
            total, difference, centre = {}, {}, {}
            for n, key in enumerate(JK):
                ends = even[key] + twice[key]
                under = ring[parity, n, rows]
                over = ends - odd[key]
                total[key] = under + over
                difference[key] = under - over
                centre[key] = middle[n, rows] + total[key]
                ring[parity, n, rows] = ends + odd[key]
                middle[n, rows] = 4.0 * even[key]
            flow = (difference[0, 0], centre[1, 0], centre[0, 1])
            results = (
                centre[0, 0], *flow, total[0, 0], centre[2, 0], centre[0, 2],
                difference[1, 0], difference[0, 1], centre[1, 1],
            )
            for f, value in enumerate(results):
                new[f, z, rows] = value
            for c in range(3):
                velocity[c, inner, rows] = flow[c]
                if step == 0:
                    velocity[c, inner, SIDE:PADDED] = flow[c]

        @pl.when(z >= 2)
        def _():
            pltpu.make_async_copy(new.at[:, z], out_hbm.at[:, z - 2], out_sem.at[z - 2]).start()

        return carry

    lax.fori_loop(0, PLANES + 2, stream_plane, 0)

    if not last:
        send_planes = [
            pltpu.make_async_copy(new.at[:, PLANES + 1], sendup_hbm.at[pl.ds(0, FIELDS)], send_sem.at[0]),
            pltpu.make_async_copy(new.at[:, 2], senddown_hbm.at[pl.ds(0, FIELDS)], send_sem.at[1]),
        ]
        for copy in send_planes:
            copy.start()

    def sample_box(slot, carry):
        above = slots_ref[slot * 3]
        row = slots_ref[slot * 3 + 1]
        column = slots_ref[slot * 3 + 2]

        @pl.when(jnp.logical_and(above > -BZ, above < PLANES))
        def _():
            here = ((lane - column) & (SIDE - 1)) < BXY
            back = (SIDE - column) & (SIDE - 1)

            def sample_plane(k, carry):
                for c in range(3):
                    cells = velocity[c, above + k, pl.ds(row, BXY)]
                    for half in range(2):
                        part = jnp.where(here, cells[half * 8 : half * 8 + 8], 0.0)
                        part = pltpu.roll(part, back, 1)
                        for bit in range(3):
                            below = pltpu.roll(part, 8 - (1 << bit), 0)
                            part = part + pltpu.roll(below, BXY << bit, 1)
                        sampled[k * 2 + half, pl.ds(slot * 3 + c, 1)] = part[0:1]
                return carry

            lax.fori_loop(jnp.maximum(0, -above), jnp.minimum(BZ, PLANES - above), sample_plane, 0)

        return carry

    lax.fori_loop(0, BLOCKS * OWNED, sample_box, 0)

    dot = functools.partial(
        lax.dot_general, dimension_numbers=(((1,), (1,)), ((), ())), preferred_element_type=F32
    )
    part_high, part_low = split(jnp.concatenate([sampled[n] for n in range(16)], axis=1))
    main = dot(jnp.concatenate([part_high, part_low], axis=0), high_ref[...])
    partial = main[:ROWS] + (main[ROWS:] + dot(part_high, low_ref[...]))

    newsum_ref[...] = partial if first else sum_ref[...] + partial
    if not last:
        newstate_ref[...] = state[...] + MOBILITY * partial
        for part in range(3):
            lanes = slice(part * 128, part * 128 + 128)
            for ref, start, owners in ((tail_up, 1, 3), (tail_down, 0, 4)):
                for owner in range(owners):
                    block, row = place(owner * 3 + part)
                    source = (start + owner) * GROUP
                    ref[block, row : row + GROUP] = partial[source : source + GROUP, lanes]
        send_tails = [
            pltpu.make_async_copy(tail_up.at[pl.ds(0, 2)], sendup_hbm.at[pl.ds(FIELDS, 2)], send_sem.at[2]),
            pltpu.make_async_copy(tail_down.at[pl.ds(0, 3)], senddown_hbm.at[pl.ds(FIELDS, 3)], send_sem.at[3]),
        ]
        for copy in send_tails:
            copy.start()
        for copy in send_planes + send_tails:
            copy.wait()
    for z in range(PLANES):
        pltpu.make_async_copy(new.at[:, z + 2], out_hbm.at[:, z], out_sem.at[z]).wait()


def advance(first, last, slots, high, low, moments, up, down, *rest):
    square = (SIDE, SIDE)
    out_shape = [
        jax.ShapeDtypeStruct((FIELDS, PLANES) + square, F32),
        jax.ShapeDtypeStruct((ROWS, LANES), F32),
    ]
    out_specs = [ANY, VMEM]
    if not last:
        out_shape += [
            jax.ShapeDtypeStruct((ROWS, LANES), F32),
            jax.ShapeDtypeStruct((FIELDS + 2,) + square, F32),
            jax.ShapeDtypeStruct((FIELDS + 3,) + square, F32),
        ]
        out_specs += [VMEM, ANY, ANY]
    scratch = [
        pltpu.VMEM((FIELDS, PLANES + 2) + square, F32),
        pltpu.VMEM((FIELDS, PLANES + 2) + square, F32),
        pltpu.VMEM((3, PLANES, PADDED, SIDE), F32),
        pltpu.VMEM((3, PLANES + 2, PADDED, SIDE), F32),
        pltpu.VMEM((CELLS // 128, ROWS, 128), F32),
        pltpu.VMEM((CELLS // 128, ROWS, 128), F32),
        pltpu.VMEM((3,) + square, F32),
        pltpu.VMEM((3,) + square, F32),
        pltpu.VMEM((15, PADDED, SIDE), F32),
        pltpu.VMEM((6,) + square, F32),
        pltpu.VMEM((2, 6) + square, F32),
        pltpu.VMEM((6,) + square, F32),
        pltpu.VMEM((ROWS, LANES), F32),
        pltpu.SemaphoreType.DMA((PLANES + 2,)),
        pltpu.SemaphoreType.DMA((2,)),
        pltpu.SemaphoreType.DMA((PLANES,)),
        pltpu.SemaphoreType.DMA((4,)),
    ]
    return pl.pallas_call(
        functools.partial(step_kernel, first, last),
        out_shape=out_shape,
        in_specs=[SMEM, VMEM, VMEM, ANY, ANY, ANY] + [VMEM] * len(rest),
        out_specs=out_specs,
        scratch_shapes=scratch,
        compiler_params=pltpu.CompilerParams(vmem_limit_bytes=48 * 2**20),
        cost_estimate=pl.CostEstimate(
            flops=4 * 10**8, bytes_accessed=16 * 2**20, transcendentals=0
        ),
        name="first_step" if first else "last_step" if last else "step",
    )(slots, high, low, moments, up, down, *rest)


def per_device(moments, shapes, anchors, synthesis, spreading):
    devices = lax.axis_size("gz")
    total_planes = PLANES * devices
    small = jnp.concatenate(
        [
            shapes.reshape(GROUP, COEFS),
            jnp.zeros((GROUP, ANCHOR_LANE - COEFS), F32),
            anchors.astype(F32).reshape(GROUP, 1),
            jnp.zeros((GROUP, LANES - ANCHOR_LANE - 1), F32),
        ],
        axis=1,
    )
    send_up, send_down = pack(moments, small)
    below2, above2 = shifted(small, 2), shifted(small, -2)
    up, down = shifted(send_up, 1), shifted(send_down, -1)
    high, low = couple(jnp.pad(synthesis, ((0, 0), (0, LANES - COEFS))), spreading)

    block, row = place(2)
    edge = ANCHOR_LANE - 256
    places = jnp.concatenate(
        [
            below2[:, ANCHOR_LANE],
            up[FIELDS + block, row : row + GROUP, edge],
            small[:, ANCHOR_LANE],
            down[FIELDS + block, row : row + GROUP, edge],
            above2[:, ANCHOR_LANE],
        ]
    ).astype(jnp.int32)
    half = total_planes // 2
    local = (places - PLANES * lax.axis_index("gz") + half) % total_planes - half
    slots = jnp.where(jnp.arange(ROWS, dtype=jnp.int32) % 3 == 0, local, places)

    rest = (small, below2, above2)
    for step in range(STEPS):
        last = step == STEPS - 1
        results = advance(step == 0, last, slots, high, low, moments, up, down, *rest)
        moments, sums = results[:2]
        if not last:
            state, send_up, send_down = results[2:]
            up, down = shifted(send_up, 1), shifted(send_down, -1)
            rest = (state, sums)

    group = [sums[i * GROUP : (i + 1) * GROUP] for i in range(BLOCKS)]
    change = group[2] + shifted(group[3], 1) + shifted(group[1], -1) + shifted(group[0], -2)
    change = change[:, :COEFS].reshape(OWNED, 3, COEFS)
    return (moments, shapes + MOBILITY * change)


def solution(mesh):
    return jax.shard_map(
        per_device,
        mesh=mesh,
        in_specs=(P(None, "gz", None, None), P("gz", None, None), P("gz", None), P(), P()),
        out_specs=(P(None, "gz", None, None), P("gz", None, None)),
        check_vma=False,
    )
```

```python
import functools

import jax
import jax.numpy as jnp
from jax import lax
from jax.experimental import pallas as pl
from jax.experimental.pallas import tpu as pltpu
from jax.sharding import PartitionSpec as P

LMAX = 16
BZ = 8
BXY = 16
STEPS = 3
STIFF_SCALE = 0.002
MOBILITY = 0.5

PLANES = 8
SIDE = 128
OWNED = 8
COEFS = 289
LANES = 384
CELLS = 2048
POINTS = 512
GROUP = OWNED * 3
BLOCKS = 5
ROWS = GROUP * BLOCKS
ANCHOR_LANE = 300
FIELDS = 10
PADDED = 144
PITCH = 145
DEPTH = PLANES + 2 * BZ
BOXED = ROWS + 1
CHUNK = 16
JK = ((0, 0), (1, 0), (2, 0), (0, 1), (1, 1), (0, 2))

ANY = pl.BlockSpec(memory_space=pl.ANY)
VMEM = pl.BlockSpec(memory_space=pltpu.VMEM)
SMEM = pl.BlockSpec(memory_space=pltpu.SMEM)
F32 = jnp.float32
BF16 = jnp.bfloat16


def shifted(block, distance):
    devices = lax.axis_size("gz")
    return lax.ppermute(block, "gz", [((i - distance) % devices, i) for i in range(devices)])


def split(value):
    high = value.astype(BF16)
    return high, (value - high.astype(F32)).astype(BF16)


def place(group):
    return group // 5, (group % 5) * GROUP


def chunk_row(n):
    return (n % 2 * 8 + n // 2) * BOXED


def couple_kernel(synthesis_ref, spreading_ref, high_ref, low_ref):
    s_high, s_low = split(synthesis_ref[...])
    w_high, w_low = split(spreading_ref[...])
    dot = functools.partial(
        lax.dot_general, dimension_numbers=(((0,), (0,)), ((), ())), preferred_element_type=F32
    )
    total = dot(s_high, w_high) + (dot(s_high, w_low) + dot(s_low, w_high))
    high, low = split(total)
    high_ref[...] = high
    low_ref[...] = low


def couple(synthesis, spreading):
    width = 512
    shape = jax.ShapeDtypeStruct((LANES, CELLS), BF16)
    return pl.pallas_call(
        couple_kernel,
        out_shape=(shape, shape),
        grid=(CELLS // width,),
        in_specs=[
            pl.BlockSpec((POINTS, LANES), lambda i: (0, 0)),
            pl.BlockSpec((POINTS, width), lambda i: (0, i)),
        ],
        out_specs=[pl.BlockSpec((LANES, width), lambda i: (0, i))] * 2,
        cost_estimate=pl.CostEstimate(
            flops=6 * LANES * POINTS * CELLS, bytes_accessed=8 * 2**20, transcendentals=0
        ),
        name="couple",
    )(synthesis, spreading)


def pack_kernel(first_ref, last_ref, small_ref, up_ref, down_ref):
    for out_ref, plane_ref in ((up_ref, last_ref), (down_ref, first_ref)):
        out_ref[0:FIELDS] = plane_ref[:, 0]
        for part in range(3):
            block, row = place(part)
            out_ref[FIELDS + block, row : row + GROUP] = small_ref[:, part * 128 : part * 128 + 128]


def pack(moments, small):
    shape = jax.ShapeDtypeStruct((FIELDS + 1, SIDE, SIDE), F32)
    whole = pl.BlockSpec((FIELDS + 1, SIDE, SIDE), lambda i: (0, 0, 0))
    return pl.pallas_call(
        pack_kernel,
        out_shape=(shape, shape),
        grid=(1,),
        in_specs=[
            pl.BlockSpec((FIELDS, 1, SIDE, SIDE), lambda i: (0, 0, 0, 0)),
            pl.BlockSpec((FIELDS, 1, SIDE, SIDE), lambda i: (0, PLANES - 1, 0, 0)),
            pl.BlockSpec((GROUP, LANES), lambda i: (0, 0)),
        ],
        out_specs=[whole, whole],
        name="pack",
    )(moments, moments, small)


def spread_x(zero, one, two):
    plus = zero if two is None else zero + two
    minus = plus
    if one is not None:
        plus, minus = plus + one, plus - one
    plus = pltpu.roll(plus, 1, 1)
    minus = pltpu.roll(minus, SIDE - 1, 1)
    both = plus + minus
    return (4.0 * zero + both, plus - minus, both)


def collide_rows(m, force):
    unit = 1.0 / 216.0
    rho = m[0]
    u = [m[1 + a] + 0.5 * force[a] for a in range(3)]
    t = [0.625 * u[a] + 0.375 * force[a] for a in range(3)]
    v = [(9.0 * unit) * u[a] for a in range(3)]
    line = [(3.0 * unit) * (m[1 + a] + force[a]) for a in range(3)]
    shared = (0.375 * unit) * rho
    square = [shared - (1.125 * unit) * m[4 + a] + v[a] * t[a] for a in range(3)]
    cross = [
        v[a] * t[b] + v[b] * t[a] - (2.25 * unit) * m[7 + n]
        for n, (a, b) in enumerate(((0, 1), (0, 2), (1, 2)))
    ]
    cell = unit * rho - (1.0 / 3.0) * (square[0] + square[1] + square[2])
    return cell, line, square, cross


def step_kernel(first, last, *refs):
    refs = list(refs)
    slots_ref = refs.pop(0)
    high_ref, low_ref, moments_hbm, up_hbm, down_hbm = refs[:5]
    del refs[:5]
    if first:
        own_ref, below_ref, above_ref = refs[:3]
        del refs[:3]
    else:
        state_ref, sum_ref = refs[:2]
        del refs[:2]
    out_hbm, newsum_ref = refs[:2]
    del refs[:2]
    if not last:
        newstate_ref, sendup_hbm, senddown_hbm = refs[:3]
        del refs[:3]
    (
        old, new, velocity, force, boxes, sampled, tail_up, tail_down,
        shifts, stills, ring, middle, state,
        in_sem, halo_sem, out_sem, send_sem,
    ) = refs

    up_blocks = up_hbm.shape[0] - FIELDS
    down_blocks = down_hbm.shape[0] - FIELDS
    fetch_tails = [
        pltpu.make_async_copy(up_hbm.at[pl.ds(FIELDS, up_blocks)], tail_up.at[pl.ds(0, up_blocks)], halo_sem.at[0]),
        pltpu.make_async_copy(down_hbm.at[pl.ds(FIELDS, down_blocks)], tail_down.at[pl.ds(0, down_blocks)], halo_sem.at[1]),
    ]
    fetch_planes = [pltpu.make_async_copy(up_hbm.at[pl.ds(0, FIELDS)], old.at[:, 0], in_sem.at[0])]
    for z in range(PLANES):
        fetch_planes.append(
            pltpu.make_async_copy(moments_hbm.at[:, z], old.at[:, z + 1], in_sem.at[z + 1])
        )
    fetch_planes.append(
        pltpu.make_async_copy(down_hbm.at[pl.ds(0, FIELDS)], old.at[:, PLANES + 1], in_sem.at[PLANES + 1])
    )
    for copy in fetch_tails:
        copy.start()
    for copy in fetch_planes:
        copy.start()

    for c in range(3):
        start = (c * DEPTH + BZ - 1) * PITCH
        force[start : start + (PLANES + 2) * PITCH] = jnp.zeros(((PLANES + 2) * PITCH, SIDE), F32)
    sampled[...] = jnp.zeros_like(sampled)
    for copy in fetch_tails:
        copy.wait()

    for part in range(3):
        lanes = slice(part * 128, part * 128 + 128)

        def tail(ref, owner):
            block, row = place(owner * 3 + part)
            return ref[block, row : row + GROUP]

        for owner in range(BLOCKS):
            rows = slice(owner * GROUP, owner * GROUP + GROUP)
            if first:
                value = (
                    below_ref[:, lanes] if owner == 0
                    else tail(tail_up, 0) if owner == 1
                    else own_ref[:, lanes] if owner == 2
                    else tail(tail_down, 0) if owner == 3
                    else above_ref[:, lanes]
                )
                if part == 2:
                    lane = lax.broadcasted_iota(jnp.int32, value.shape, 1)
                    value = jnp.where(lane < COEFS - 256, value, 0.0)
            else:
                value = state_ref[rows, lanes]
                if owner < 3:
                    value = value + MOBILITY * tail(tail_up, owner)
                if owner > 0:
                    value = value + MOBILITY * tail(tail_down, owner - 1)
            state[rows, lanes] = value

    number = lax.broadcasted_iota(jnp.int32, (1, LANES), 1)
    degree = jnp.zeros((1, LANES), jnp.int32)
    for step in range(1, LMAX + 1):
        degree = degree + (number >= step * step).astype(jnp.int32)
    stiffness = STIFF_SCALE * (degree * (degree + 1) + 2).astype(F32)
    coef_high, coef_low = split(-stiffness * state[...])
    both = jnp.concatenate([coef_high, coef_low], axis=0)
    for part in range(CELLS // 512):
        lanes = slice(part * 512, part * 512 + 512)
        main = jnp.dot(both, high_ref[:, lanes], preferred_element_type=F32)
        rest = jnp.dot(coef_high, low_ref[:, lanes], preferred_element_type=F32)
        whole = main[:ROWS] + (main[ROWS:] + rest)
        for chunk in range(4):
            start = chunk_row(part * 4 + chunk)
            boxes[start : start + ROWS] = whole[:, chunk * 128 : chunk * 128 + 128]

    def box_parts(slot):
        above = slots_ref[slot * 3]
        row = slots_ref[slot * 3 + 1]
        column = slots_ref[slot * 3 + 2]
        lane = lax.broadcasted_iota(jnp.int32, (BXY, SIDE), 1)
        inside = lax.broadcasted_iota(jnp.int32, (BXY, SIDE), 0)
        hit = (((lane - column) & (SIDE - 1)) == inside).astype(F32).astype(BF16)
        none = jnp.zeros((BXY, SIDE), BF16)
        spots = jnp.concatenate(
            [jnp.concatenate([hit if i == n else none for i in range(8)], axis=1) for n in range(8)],
            axis=0,
        )
        starts = [
            (c * DEPTH + above + BZ) * PITCH + row + half * 8 for c in range(3) for half in range(2)
        ]
        rows = [half * 8 * BOXED + slot * 3 + c for c in range(3) for half in range(2)]
        return above, spots, starts, rows

    def place_box(slot, carry):
        @pl.when(jnp.logical_and(slots_ref[slot * 3] >= -BZ, slots_ref[slot * 3] <= PLANES))
        def _():
            above, spots, starts, rows = box_parts(slot)
            cells = jnp.concatenate([boxes[pl.ds(start, 8, stride=BOXED)] for start in rows], axis=0)
            placed = jnp.dot(
                jnp.concatenate(split(cells), axis=1),
                jnp.concatenate([spots, spots], axis=0),
                preferred_element_type=F32,
            )
            where = [
                (pl.ds(start + i, 8, stride=PITCH), slice(n * 8, n * 8 + 8), slice(i * 128, i * 128 + 128))
                for n, start in enumerate(starts)
                for i in range(8)
            ]
            sums = [force[there] + placed[here, lanes] for there, here, lanes in where]
            for (there, here, lanes), value in zip(where, sums):
                force[there] = value

        return carry

    lax.fori_loop(0, BLOCKS * OWNED, place_box, 0)

    def fold(z, carry):
        for c in range(3):
            start = (c * DEPTH + z + BZ - 1) * PITCH
            first = pl.ds(start, BXY)
            force[first] = force[first] + force[pl.ds(start + SIDE, BXY)]
        return carry

    lax.fori_loop(0, PLANES + 2, fold, 0)

    def stream_plane(z, carry):
        pltpu.make_async_copy(moments_hbm.at[:, 0], old.at[:, z], in_sem.at[z]).wait()

        def collide_chunk(step, carry):
            y = pl.multiple_of(step * CHUNK, CHUNK)
            rows = pl.ds(y, CHUNK)
            m = [old[f, z, rows] for f in range(FIELDS)]
            cell, line, square, cross = collide_rows(
                m, [force[pl.ds((c * DEPTH + z + BZ - 1) * PITCH + y, CHUNK)] for c in range(3)]
            )
            even = [
                spread_x(cell, line[2], square[2]),
                spread_x(line[1], cross[2], None),
                spread_x(square[1], None, None),
            ]
            twice = spread_x(square[0], None, None)
            odd = [spread_x(line[0], cross[1], None), spread_x(cross[0], None, None)]
            moved = pl.ds(y + 8, CHUNK)
            for k in range(3):
                ends = even[0][k] + even[2][k]
                shifts[k, moved] = ends + even[1][k]
                shifts[3 + k, moved] = ends - even[1][k]
                shifts[6 + k, moved] = odd[0][k] + odd[1][k]
                shifts[9 + k, moved] = odd[0][k] - odd[1][k]
                shifts[12 + k, moved] = twice[k]
                stills[k, rows] = 4.0 * even[0][k]
                stills[3 + k, rows] = 4.0 * odd[0][k]
            return carry

        lax.fori_loop(0, SIDE // CHUNK, collide_chunk, 0)
        for field in range(15):
            shifts[field, 7:8] = shifts[field, SIDE + 7 : SIDE + 8]
            shifts[field, SIDE + 8 : SIDE + 9] = shifts[field, 8:9]
        parity = z % 2
        inner = jnp.clip(z - 2, 0, PLANES - 1)

        for step in range(SIDE // CHUNK):
            y = step * CHUNK
            rows = slice(y, y + CHUNK)
            after = slice(y + 7, y + 7 + CHUNK)
            before = slice(y + 9, y + 9 + CHUNK)
            even, odd, twice = {}, {}, {}
            for k in range(3):
                for target, plus, minus, still in (
                    (even, k, 3 + k, lambda k=k: stills[k, rows]),
                    (odd, 6 + k, 9 + k, lambda k=k: stills[3 + k, rows]),
                    (twice, 12 + k, 12 + k, lambda k=k: 4.0 * shifts[12 + k, y + 8 : y + 8 + CHUNK]),
                ):
                    up, down = shifts[plus, after], shifts[minus, before]
                    both = up + down
                    target[0, k] = still() + both
                    if k < 2:
                        target[1, k] = up - down
                    if k < 1:
                        target[2, k] = both
            total, difference, centre = {}, {}, {}
            for n, key in enumerate(JK):
                ends = even[key] + twice[key]
                under = ring[parity, n, rows]
                over = ends - odd[key]
                total[key] = under + over
                difference[key] = under - over
                centre[key] = middle[n, rows] + total[key]
                ring[parity, n, rows] = ends + odd[key]
                middle[n, rows] = 4.0 * even[key]
            flow = (difference[0, 0], centre[1, 0], centre[0, 1])
            results = (
                centre[0, 0], *flow, total[0, 0], centre[2, 0], centre[0, 2],
                difference[1, 0], difference[0, 1], centre[1, 1],
            )
            for f, value in enumerate(results):
                new[f, z, rows] = value
            for c in range(3):
                start = (c * DEPTH + inner + BZ) * PITCH
                velocity[pl.ds(start + y, CHUNK)] = flow[c]
                if step == 0:
                    velocity[pl.ds(start + SIDE, BXY)] = flow[c]

        @pl.when(z >= 2)
        def _():
            pltpu.make_async_copy(new.at[:, z], out_hbm.at[:, z - 2], out_sem.at[z - 2]).start()

        return carry

    lax.fori_loop(0, PLANES + 2, stream_plane, 0)

    if not last:
        send_planes = [
            pltpu.make_async_copy(new.at[:, PLANES + 1], sendup_hbm.at[pl.ds(0, FIELDS)], send_sem.at[0]),
            pltpu.make_async_copy(new.at[:, 2], senddown_hbm.at[pl.ds(0, FIELDS)], send_sem.at[1]),
        ]
        for copy in send_planes:
            copy.start()

    across = functools.partial(
        lax.dot_general, dimension_numbers=(((1,), (1,)), ((), ())), preferred_element_type=F32
    )

    def sample_box(slot, carry):
        @pl.when(jnp.logical_and(slots_ref[slot * 3] > -BZ, slots_ref[slot * 3] < PLANES))
        def _():
            above, spots, starts, rows = box_parts(slot)
            cells = jnp.concatenate(
                [
                    jnp.concatenate([velocity[pl.ds(start + i, 8, stride=PITCH)] for i in range(8)], axis=1)
                    for start in starts
                ],
                axis=0,
            )
            found = across(jnp.concatenate(split(cells), axis=0), spots)
            plane = lax.broadcasted_iota(jnp.int32, (8, SIDE), 0) + above
            ours = jnp.logical_and(plane >= 0, plane < PLANES)
            for n, start in enumerate(rows):
                value = found[n * 8 : n * 8 + 8] + found[48 + n * 8 : 56 + n * 8]
                sampled[pl.ds(start, 8, stride=BOXED)] = jnp.where(ours, value, 0.0)

        return carry

    lax.fori_loop(0, BLOCKS * OWNED, sample_box, 0)

    part_high, part_low = split(
        jnp.concatenate([sampled[chunk_row(n) : chunk_row(n) + ROWS] for n in range(16)], axis=1)
    )
    main = across(jnp.concatenate([part_high, part_low], axis=0), high_ref[...])
    partial = main[:ROWS] + (main[ROWS:] + across(part_high, low_ref[...]))

    newsum_ref[...] = partial if first else sum_ref[...] + partial
    if not last:
        newstate_ref[...] = state[...] + MOBILITY * partial
        for part in range(3):
            lanes = slice(part * 128, part * 128 + 128)
            for ref, start, owners in ((tail_up, 1, 3), (tail_down, 0, 4)):
                for owner in range(owners):
                    block, row = place(owner * 3 + part)
                    source = (start + owner) * GROUP
                    ref[block, row : row + GROUP] = partial[source : source + GROUP, lanes]
        send_tails = [
            pltpu.make_async_copy(tail_up.at[pl.ds(0, 2)], sendup_hbm.at[pl.ds(FIELDS, 2)], send_sem.at[2]),
            pltpu.make_async_copy(tail_down.at[pl.ds(0, 3)], senddown_hbm.at[pl.ds(FIELDS, 3)], send_sem.at[3]),
        ]
        for copy in send_tails:
            copy.start()
        for copy in send_planes + send_tails:
            copy.wait()
    for z in range(PLANES):
        pltpu.make_async_copy(new.at[:, z + 2], out_hbm.at[:, z], out_sem.at[z]).wait()


def advance(first, last, slots, high, low, moments, up, down, *rest):
    square = (SIDE, SIDE)
    out_shape = [
        jax.ShapeDtypeStruct((FIELDS, PLANES) + square, F32),
        jax.ShapeDtypeStruct((ROWS, LANES), F32),
    ]
    out_specs = [ANY, VMEM]
    if not last:
        out_shape += [
            jax.ShapeDtypeStruct((ROWS, LANES), F32),
            jax.ShapeDtypeStruct((FIELDS + 2,) + square, F32),
            jax.ShapeDtypeStruct((FIELDS + 3,) + square, F32),
        ]
        out_specs += [VMEM, ANY, ANY]
    scratch = [
        pltpu.VMEM((FIELDS, PLANES + 2) + square, F32),
        pltpu.VMEM((FIELDS, PLANES + 2) + square, F32),
        pltpu.VMEM((3 * DEPTH * PITCH, SIDE), F32),
        pltpu.VMEM((3 * DEPTH * PITCH, SIDE), F32),
        pltpu.VMEM((CELLS // 128 * BOXED, 128), F32),
        pltpu.VMEM((CELLS // 128 * BOXED, 128), F32),
        pltpu.VMEM((3,) + square, F32),
        pltpu.VMEM((3,) + square, F32),
        pltpu.VMEM((15, PADDED, SIDE), F32),
        pltpu.VMEM((6,) + square, F32),
        pltpu.VMEM((2, 6) + square, F32),
        pltpu.VMEM((6,) + square, F32),
        pltpu.VMEM((ROWS, LANES), F32),
        pltpu.SemaphoreType.DMA((PLANES + 2,)),
        pltpu.SemaphoreType.DMA((2,)),
        pltpu.SemaphoreType.DMA((PLANES,)),
        pltpu.SemaphoreType.DMA((4,)),
    ]
    return pl.pallas_call(
        functools.partial(step_kernel, first, last),
        out_shape=out_shape,
        in_specs=[SMEM, VMEM, VMEM, ANY, ANY, ANY] + [VMEM] * len(rest),
        out_specs=out_specs,
        scratch_shapes=scratch,
        compiler_params=pltpu.CompilerParams(vmem_limit_bytes=48 * 2**20),
        cost_estimate=pl.CostEstimate(
            flops=4 * 10**8, bytes_accessed=16 * 2**20, transcendentals=0
        ),
        name="first_step" if first else "last_step" if last else "step",
    )(slots, high, low, moments, up, down, *rest)


def per_device(moments, shapes, anchors, synthesis, spreading):
    devices = lax.axis_size("gz")
    total_planes = PLANES * devices
    small = jnp.concatenate(
        [
            shapes.reshape(GROUP, COEFS),
            jnp.zeros((GROUP, ANCHOR_LANE - COEFS), F32),
            anchors.astype(F32).reshape(GROUP, 1),
            jnp.zeros((GROUP, LANES - ANCHOR_LANE - 1), F32),
        ],
        axis=1,
    )
    send_up, send_down = pack(moments, small)
    below2, above2 = shifted(small, 2), shifted(small, -2)
    up, down = shifted(send_up, 1), shifted(send_down, -1)
    high, low = couple(jnp.pad(synthesis, ((0, 0), (0, LANES - COEFS))), spreading)

    block, row = place(2)
    edge = ANCHOR_LANE - 256
    places = jnp.concatenate(
        [
            below2[:, ANCHOR_LANE],
            up[FIELDS + block, row : row + GROUP, edge],
            small[:, ANCHOR_LANE],
            down[FIELDS + block, row : row + GROUP, edge],
            above2[:, ANCHOR_LANE],
        ]
    ).astype(jnp.int32)
    half = total_planes // 2
    local = (places - PLANES * lax.axis_index("gz") + half) % total_planes - half
    slots = jnp.where(jnp.arange(ROWS, dtype=jnp.int32) % 3 == 0, local, places)

    rest = (small, below2, above2)
    for step in range(STEPS):
        last = step == STEPS - 1
        results = advance(step == 0, last, slots, high, low, moments, up, down, *rest)
        moments, sums = results[:2]
        if not last:
            state, send_up, send_down = results[2:]
            up, down = shifted(send_up, 1), shifted(send_down, -1)
            rest = (state, sums)

    group = [sums[i * GROUP : (i + 1) * GROUP] for i in range(BLOCKS)]
    change = group[2] + shifted(group[3], 1) + shifted(group[1], -1) + shifted(group[0], -2)
    change = change[:, :COEFS].reshape(OWNED, 3, COEFS)
    return (moments, shapes + MOBILITY * change)


def solution(mesh):
    return jax.shard_map(
        per_device,
        mesh=mesh,
        in_specs=(P(None, "gz", None, None), P("gz", None, None), P("gz", None), P(), P()),
        out_specs=(P(None, "gz", None, None), P("gz", None, None)),
        check_vma=False,
    )
```

```python
import functools

import jax
import jax.numpy as jnp
from jax import lax
from jax.experimental import pallas as pl
from jax.experimental.pallas import tpu as pltpu
from jax.sharding import PartitionSpec as P


LMAX = 16
BZ = 8
BXY = 16
STEPS = 3
STIFF_SCALE = 0.002
MOBILITY = 0.5

PLANES = 8
SIDE = 128
OWNED = 8
COEFS = 289
SLOTS = 40
LANES = 384
KEPT = 304
CELLS = 2048
POINTS = 512
GROUP = OWNED * 3
BLOCKS = 5
ROWS = GROUP * BLOCKS
ANCHOR_LANE = 300
FIELDS = 10
SENT = 9 * SIDE
NARROW = COEFS - 256
STEP_LANES = 40
PADDED = 144
PITCH = 145
DEPTH = PLANES + 2 * BZ + 1
BOXED = ROWS + 1
CHUNK = 16
JK = ((0, 0), (1, 0), (2, 0), (0, 1), (1, 1), (0, 2))

VMEM = pl.BlockSpec(memory_space=pltpu.VMEM)
SMEM = pl.BlockSpec(memory_space=pltpu.SMEM)
HBM = pl.BlockSpec(memory_space=pltpu.HBM)
F32 = jnp.float32
BF16 = jnp.bfloat16


def shifted(block, distance):
    devices = lax.axis_size("gz")
    return lax.ppermute(block, "gz", [((i - distance) % devices, i) for i in range(devices)])


def split(value):
    high = value.astype(BF16)
    return high, (value - high.astype(F32)).astype(BF16)


def tail_rows(owner, part, owners):
    if part < 2:
        group, lane = owner * 2 + part, 0
    else:
        group, lane = owners * 2 + owner // 3, STEP_LANES * (owner % 3)
    start = SENT + group * GROUP
    return slice(start, start + GROUP), lane


def message_rows(owners):
    return SENT + (owners * 2 + (owners + 2) // 3) * GROUP


def read_tail(ref, owner, part, owners):
    rows, lane = tail_rows(owner, part, owners)
    value = ref[rows]
    if part == 2:
        if lane:
            value = pltpu.roll(value, 128 - lane, 1)
        lanes = lax.broadcasted_iota(jnp.int32, value.shape, 1)
        value = jnp.where(lanes < NARROW, value, 0.0)
    return value


def write_tail(ref, values, width):
    owners = values
    for owner in range(owners):
        for part in range(2):
            ref[tail_rows(owner, part, owners)[0]] = width(owner, part)
    for first in range(0, owners, 3):
        packed = width(first, 2)
        for owner in range(first + 1, min(first + 3, owners)):
            packed = packed + pltpu.roll(width(owner, 2), STEP_LANES * (owner - first), 1)
        ref[tail_rows(first, 2, owners)[0]] = packed


def write_plane(ref, field):
    trace = field(4)
    values = [field(0) - 0.6 * trace, field(1), field(2), field(3)]
    values += [field(5) - 0.2 * trace, field(6) - 0.2 * trace, field(7), field(8), field(9)]
    for n, value in enumerate(values):
        ref[n * SIDE : n * SIDE + SIDE] = value


def slot_row(slot):
    return slot + (slot // OWNED) * (2 * OWNED)


def chunk_row(n):
    return (n % 2 * 8 + n // 2) * BOXED


def couple_kernel(synthesis_ref, spreading_ref, high_ref, low_ref):
    width = 512
    turned = jnp.concatenate(split(synthesis_ref[...].T[0:KEPT]), axis=0)
    for ref in (high_ref, low_ref):
        ref[KEPT:] = jnp.zeros((LANES - KEPT, CELLS), BF16)
    for first in range(0, CELLS, width):
        lanes = slice(first, first + width)
        w_high, w_low = split(spreading_ref[:, lanes])
        main = jnp.dot(turned, w_high, preferred_element_type=F32)
        rest = jnp.dot(turned[0:KEPT], w_low, preferred_element_type=F32)
        high_ref[0:KEPT, lanes], low_ref[0:KEPT, lanes] = split(main[:KEPT] + (main[KEPT:] + rest))


def couple(synthesis, spreading):
    shape = jax.ShapeDtypeStruct((LANES, CELLS), BF16)
    return pl.pallas_call(
        couple_kernel,
        out_shape=(shape, shape),
        in_specs=[VMEM, VMEM],
        out_specs=[VMEM, VMEM],
        compiler_params=pltpu.CompilerParams(vmem_limit_bytes=32 * 2**20),
        cost_estimate=pl.CostEstimate(
            flops=6 * LANES * POINTS * CELLS, bytes_accessed=8 * 2**20, transcendentals=0
        ),
        name="couple",
    )(synthesis, spreading)


def pack_kernel(anchors_ref, moments_hbm, shapes_ref, small_ref, up_ref, down_ref, planes, sem):
    copies = [
        pltpu.make_async_copy(moments_hbm.at[:, z], planes.at[n], sem.at[n])
        for n, z in enumerate((PLANES - 1, 0))
    ]
    for copy in copies:
        copy.start()
    small_ref[...] = jnp.zeros_like(small_ref)
    for c in range(3):
        small_ref[c * OWNED : c * OWNED + OWNED, 0:COEFS] = shapes_ref[c]
    part = small_ref[:, 256:LANES]
    row = lax.broadcasted_iota(jnp.int32, part.shape, 0)
    anchor = jnp.zeros(part.shape, jnp.int32)
    for n in range(GROUP):
        anchor = jnp.where(row == n, anchors_ref[n // OWNED, n % OWNED], anchor)
    lane = lax.broadcasted_iota(jnp.int32, part.shape, 1)
    part = jnp.where(lane == ANCHOR_LANE - 256, anchor.astype(F32), part)
    small_ref[:, 256:LANES] = part
    for ref in (up_ref, down_ref):
        write_tail(ref, 1, lambda owner, p: small_ref[:, p * 128 : p * 128 + 128])
    for n, ref in enumerate((up_ref, down_ref)):
        copies[n].wait()
        write_plane(ref, lambda f, n=n: planes[n, f])


def pack(moments, shapes, anchors):
    shape = jax.ShapeDtypeStruct((message_rows(1), SIDE), F32)
    return pl.pallas_call(
        pack_kernel,
        out_shape=(jax.ShapeDtypeStruct((GROUP, LANES), F32), shape, shape),
        in_specs=[SMEM, HBM, VMEM],
        out_specs=[VMEM, VMEM, VMEM],
        scratch_shapes=[pltpu.VMEM((2, FIELDS, SIDE, SIDE), F32), pltpu.SemaphoreType.DMA((2,))],
        compiler_params=pltpu.CompilerParams(vmem_limit_bytes=60 * 2**20),
        name="pack",
    )(anchors, moments, shapes)


def spread_x(zero, one, two):
    plus = zero if two is None else zero + two
    minus = plus
    if one is not None:
        plus, minus = plus + one, plus - one
    plus = pltpu.roll(plus, 1, 1)
    minus = pltpu.roll(minus, SIDE - 1, 1)
    both = plus + minus
    return (4.0 * zero + both, plus - minus, both)


def collide_rows(m, force):
    unit = 1.0 / 216.0
    rho = m[0]
    u = [m[1 + a] + 0.5 * force[a] for a in range(3)]
    t = [0.625 * u[a] + 0.375 * force[a] for a in range(3)]
    v = [(9.0 * unit) * u[a] for a in range(3)]
    line = [(3.0 * unit) * (m[1 + a] + force[a]) for a in range(3)]
    shared = (0.375 * unit) * rho
    square = [shared - (1.125 * unit) * m[4 + a] + v[a] * t[a] for a in range(3)]
    cross = [
        v[a] * t[b] + v[b] * t[a] - (2.25 * unit) * m[7 + n]
        for n, (a, b) in enumerate(((0, 1), (0, 2), (1, 2)))
    ]
    cell = unit * rho - (1.0 / 3.0) * (square[0] + square[1] + square[2])
    return cell, line, square, cross


def step_kernel(first, last, *refs):
    refs = list(refs)

    def take(count):
        taken = refs[:count]
        del refs[:count]
        return taken

    slots_ref, high_ref, low_ref, moments_hbm, up_ref, down_ref = take(6)
    if first:
        own_ref, below_ref, above_ref = take(3)
    else:
        state_ref, sum_ref, order_ref = take(3)
    out_hbm, newsum_ref = take(2)
    if not last:
        newstate_ref, sendup_ref, senddown_ref = take(3)
    if first:
        (order_ref,) = take(1)
    (
        old, new, velocity, force, boxes, sampled,
        shifts, stills, ring, middle, state,
        in_sem, out_sem,
    ) = refs

    for z in range(PLANES):
        pltpu.make_async_copy(moments_hbm.at[:, z], old.at[:, z + 1], in_sem.at[z]).start()

    if first:

        def scan(slot, carry):
            count, spare = carry
            above = slots_ref[slot_row(slot)]
            near = jnp.logical_and(above >= -BZ, above <= PLANES)

            @pl.when(near)
            def _():
                order_ref[count] = slot

            return count + near.astype(jnp.int32), jnp.where(near, spare, slot)

        count, spare = lax.fori_loop(0, SLOTS, scan, (jnp.int32(0), jnp.int32(0)))
        order_ref[count] = spare
        order_ref[SLOTS + 1] = (count + 1) // 2
    pairs = order_ref[SLOTS + 1]

    for c in range(3):
        start = (c * DEPTH + BZ - 1) * PITCH
        force[start : start + (PLANES + 2) * PITCH] = jnp.zeros(((PLANES + 2) * PITCH, SIDE), F32)
    sampled[...] = jnp.zeros_like(sampled)
    for ref, edge in ((up_ref, 0), (down_ref, PLANES + 1)):
        for n, f in enumerate((0, 1, 2, 3, 5, 6, 7, 8, 9)):
            old[f, edge] = ref[n * SIDE : n * SIDE + SIDE]
        old[4, edge] = jnp.zeros((SIDE, SIDE), F32)

    for part in range(3):
        lanes = slice(part * 128, part * 128 + 128)
        for owner in range(BLOCKS):
            rows = slice(owner * GROUP, owner * GROUP + GROUP)
            if first:
                if owner % 2 == 1:
                    value = read_tail(up_ref if owner == 1 else down_ref, 0, part, 1)
                else:
                    value = (below_ref, own_ref, above_ref)[owner // 2][:, lanes]
                    if part == 2:
                        lane = lax.broadcasted_iota(jnp.int32, value.shape, 1)
                        value = jnp.where(lane < NARROW, value, 0.0)
            else:
                value = state_ref[rows, lanes]
                if owner < 3:
                    value = value + MOBILITY * read_tail(up_ref, owner, part, 3)
                if owner > 0:
                    value = value + MOBILITY * read_tail(down_ref, owner - 1, part, 4)
            state[rows, lanes] = value

    number = lax.broadcasted_iota(jnp.int32, (1, LANES), 1)
    degree = jnp.zeros((1, LANES), jnp.int32)
    for step in range(1, LMAX + 1):
        degree = degree + (number >= step * step).astype(jnp.int32)
    stiffness = STIFF_SCALE * (degree * (degree + 1) + 2).astype(F32)
    coef_high, coef_low = split(-stiffness * state[...])
    both = jnp.concatenate([coef_high, coef_low], axis=0)
    for part in range(CELLS // 512):
        lanes = slice(part * 512, part * 512 + 512)
        main = jnp.dot(both, high_ref[:, lanes], preferred_element_type=F32)
        rest = jnp.dot(coef_high, low_ref[:, lanes], preferred_element_type=F32)
        whole = main[:ROWS] + (main[ROWS:] + rest)
        for chunk in range(4):
            start = chunk_row(part * 4 + chunk)
            boxes[start : start + ROWS] = whole[:, chunk * 128 : chunk * 128 + 128]

    def box_parts(slot):
        base = slot_row(slot)
        above = slots_ref[base]
        near = jnp.logical_and(above >= -BZ, above <= PLANES)
        above = jnp.where(near, above, PLANES + 1)
        row = slots_ref[base + OWNED]
        column = slots_ref[base + 2 * OWNED]
        lane = lax.broadcasted_iota(jnp.int32, (BXY, SIDE), 1)
        inside = lax.broadcasted_iota(jnp.int32, (BXY, SIDE), 0)
        hit = (((lane - column) & (SIDE - 1)) == inside).astype(F32).astype(BF16)
        none = jnp.zeros((BXY, SIDE), BF16)
        spots = jnp.concatenate(
            [jnp.concatenate([hit if i == n else none for i in range(8)], axis=1) for n in range(8)],
            axis=0,
        )
        starts = [
            (c * DEPTH + above + BZ) * PITCH + row + half * 8 for c in range(3) for half in range(2)
        ]
        rows = [half * 8 * BOXED + base + c * OWNED for c in range(3) for half in range(2)]
        return above, spots, starts, rows

    def place_pair(pair, carry):
        found = []
        for n in range(2):
            _, spots, starts, rows = box_parts(order_ref[pair * 2 + n])
            cells = jnp.concatenate([boxes[pl.ds(start, 8, stride=BOXED)] for start in rows], axis=0)
            placed = jnp.dot(
                jnp.concatenate(split(cells), axis=1),
                jnp.concatenate([spots, spots], axis=0),
                preferred_element_type=F32,
            )
            found.append((starts, placed))
        for starts, placed in found:
            where = [
                (pl.ds(start + i, 8, stride=PITCH), slice(n * 8, n * 8 + 8), slice(i * 128, i * 128 + 128))
                for n, start in enumerate(starts)
                for i in range(8)
            ]
            sums = [force[there] + placed[here, lanes] for there, here, lanes in where]
            for (there, here, lanes), value in zip(where, sums):
                force[there] = value
        return carry

    lax.fori_loop(0, pairs, place_pair, 0)

    def fold(z, carry):
        for c in range(3):
            start = (c * DEPTH + z + BZ - 1) * PITCH
            first = pl.ds(start, BXY)
            force[first] = force[first] + force[pl.ds(start + SIDE, BXY)]
        return carry

    lax.fori_loop(0, PLANES + 2, fold, 0)

    def stream_plane(z, carry):
        @pl.when(jnp.logical_and(z >= 1, z <= PLANES))
        def _():
            pltpu.make_async_copy(moments_hbm.at[:, 0], old.at[:, z], in_sem.at[z - 1]).wait()


        def collide_chunk(step, carry):
            y = pl.multiple_of(step * CHUNK, CHUNK)
            rows = pl.ds(y, CHUNK)
            m = [old[f, z, rows] for f in range(FIELDS)]
            cell, line, square, cross = collide_rows(
                m, [force[pl.ds((c * DEPTH + z + BZ - 1) * PITCH + y, CHUNK)] for c in range(3)]
            )
            even = [
                spread_x(cell, line[2], square[2]),
                spread_x(line[1], cross[2], None),
                spread_x(square[1], None, None),
            ]
            twice = spread_x(square[0], None, None)
            odd = [spread_x(line[0], cross[1], None), spread_x(cross[0], None, None)]
            moved = pl.ds(y + 8, CHUNK)
            for k in range(3):
                ends = even[0][k] + even[2][k]
                shifts[k, moved] = ends + even[1][k]
                shifts[3 + k, moved] = ends - even[1][k]
                shifts[6 + k, moved] = odd[0][k] + odd[1][k]
                shifts[9 + k, moved] = odd[0][k] - odd[1][k]
                shifts[12 + k, moved] = twice[k]
                stills[k, rows] = 4.0 * even[0][k]
                stills[3 + k, rows] = 4.0 * odd[0][k]
            return carry

        lax.fori_loop(0, SIDE // CHUNK, collide_chunk, 0)
        for field in range(15):
            shifts[field, 7:8] = shifts[field, SIDE + 7 : SIDE + 8]
            shifts[field, SIDE + 8 : SIDE + 9] = shifts[field, 8:9]
        parity = z % 2
        inner = jnp.clip(z - 2, 0, PLANES - 1)

        for step in range(SIDE // CHUNK):
            y = step * CHUNK
            rows = slice(y, y + CHUNK)
            after = slice(y + 7, y + 7 + CHUNK)
            before = slice(y + 9, y + 9 + CHUNK)
            even, odd, twice = {}, {}, {}
            for k in range(3):
                for target, plus, minus, still in (
                    (even, k, 3 + k, lambda k=k: stills[k, rows]),
                    (odd, 6 + k, 9 + k, lambda k=k: stills[3 + k, rows]),
                    (twice, 12 + k, 12 + k, lambda k=k: 4.0 * shifts[12 + k, y + 8 : y + 8 + CHUNK]),
                ):
                    up, down = shifts[plus, after], shifts[minus, before]
                    both = up + down
                    target[0, k] = still() + both
                    if k < 2:
                        target[1, k] = up - down
                    if k < 1:
                        target[2, k] = both
            total, difference, centre = {}, {}, {}
            for n, key in enumerate(JK):
                ends = even[key] + twice[key]
                under = ring[parity, n, rows]
                over = ends - odd[key]
                total[key] = under + over
                difference[key] = under - over
                centre[key] = middle[n, rows] + total[key]
                ring[parity, n, rows] = ends + odd[key]
                middle[n, rows] = 4.0 * even[key]
            flow = (difference[0, 0], centre[1, 0], centre[0, 1])
            results = (
                centre[0, 0], *flow, total[0, 0], centre[2, 0], centre[0, 2],
                difference[1, 0], difference[0, 1], centre[1, 1],
            )
            for f, value in enumerate(results):
                new[f, z, rows] = value
            for c in range(3):
                start = (c * DEPTH + inner + BZ) * PITCH
                velocity[pl.ds(start + y, CHUNK)] = flow[c]
                if step == 0:
                    velocity[pl.ds(start + SIDE, BXY)] = flow[c]

        @pl.when(z >= 2)
        def _():
            pltpu.make_async_copy(new.at[:, z], out_hbm.at[:, z - 2], out_sem.at[z - 2]).start()

        return carry

    lax.fori_loop(0, PLANES + 2, stream_plane, 0)

    if not last:
        write_plane(sendup_ref, lambda f: new[f, PLANES + 1])
        write_plane(senddown_ref, lambda f: new[f, 2])

    across = functools.partial(
        lax.dot_general, dimension_numbers=(((1,), (1,)), ((), ())), preferred_element_type=F32
    )

    def sample_pair(pair, carry):
        results = []
        for n in range(2):
            above, spots, starts, rows = box_parts(order_ref[pair * 2 + n])
            cells = jnp.concatenate(
                [
                    jnp.concatenate([velocity[pl.ds(start + i, 8, stride=PITCH)] for i in range(8)], axis=1)
                    for start in starts
                ],
                axis=0,
            )
            results.append((above, rows, across(jnp.concatenate(split(cells), axis=0), spots)))
        for above, rows, found in results:
            plane = lax.broadcasted_iota(jnp.int32, (8, SIDE), 0) + above
            ours = jnp.logical_and(plane >= 0, plane < PLANES)
            for n, start in enumerate(rows):
                value = found[n * 8 : n * 8 + 8] + found[48 + n * 8 : 56 + n * 8]
                sampled[pl.ds(start, 8, stride=BOXED)] = jnp.where(ours, value, 0.0)
        return carry

    lax.fori_loop(0, pairs, sample_pair, 0)

    part_high, part_low = split(
        jnp.concatenate([sampled[chunk_row(n) : chunk_row(n) + ROWS] for n in range(16)], axis=1)
    )
    main = across(jnp.concatenate([part_high, part_low], axis=0), high_ref[...])
    partial = main[:ROWS] + (main[ROWS:] + across(part_high, low_ref[...]))

    newsum_ref[...] = partial if first else sum_ref[...] + partial
    if not last:
        newstate_ref[...] = state[...] + MOBILITY * partial
        for ref, start, owners in ((sendup_ref, GROUP, 3), (senddown_ref, 0, 4)):
            write_tail(
                ref,
                owners,
                lambda owner, part: partial[
                    start + owner * GROUP : start + owner * GROUP + GROUP, part * 128 : part * 128 + 128
                ],
            )
    for z in range(PLANES):
        pltpu.make_async_copy(new.at[:, z + 2], out_hbm.at[:, z], out_sem.at[z]).wait()


def advance(first, last, slots, high, low, moments, up, down, *rest):
    square = (SIDE, SIDE)
    out_shape = [
        jax.ShapeDtypeStruct((FIELDS, PLANES) + square, F32),
        jax.ShapeDtypeStruct((ROWS, LANES), F32),
    ]
    out_specs = [HBM, VMEM]
    if not last:
        out_shape += [
            jax.ShapeDtypeStruct((ROWS, LANES), F32),
            jax.ShapeDtypeStruct((message_rows(3), SIDE), F32),
            jax.ShapeDtypeStruct((message_rows(4), SIDE), F32),
        ]
        out_specs += [VMEM] * 3
    if first:
        out_shape.append(jax.ShapeDtypeStruct((SLOTS + 2,), jnp.int32))
        out_specs.append(SMEM)
    scratch = [
        pltpu.VMEM((FIELDS, PLANES + 2) + square, F32),
        pltpu.VMEM((FIELDS, PLANES + 2) + square, F32),
        pltpu.VMEM((3 * DEPTH * PITCH, SIDE), F32),
        pltpu.VMEM((3 * DEPTH * PITCH, SIDE), F32),
        pltpu.VMEM((CELLS // 128 * BOXED, 128), F32),
        pltpu.VMEM((CELLS // 128 * BOXED, 128), F32),
        pltpu.VMEM((15, PADDED, SIDE), F32),
        pltpu.VMEM((6,) + square, F32),
        pltpu.VMEM((2, 6) + square, F32),
        pltpu.VMEM((6,) + square, F32),
        pltpu.VMEM((ROWS, LANES), F32),
        pltpu.SemaphoreType.DMA((PLANES,)),
        pltpu.SemaphoreType.DMA((PLANES,)),
    ]
    return pl.pallas_call(
        functools.partial(step_kernel, first, last),
        out_shape=out_shape,
        in_specs=[SMEM, VMEM, VMEM, HBM, VMEM, VMEM] + [VMEM] * 2 + [VMEM if first else SMEM],
        out_specs=out_specs,
        scratch_shapes=scratch,
        compiler_params=pltpu.CompilerParams(vmem_limit_bytes=44 * 2**20),
        cost_estimate=pl.CostEstimate(
            flops=4 * 10**8, bytes_accessed=16 * 2**20, transcendentals=0
        ),
        input_output_aliases={} if first else {3: 0},
        name="first_step" if first else "last_step" if last else "step",
    )(slots, high, low, moments, up, down, *rest)


def per_device(moments, shapes, anchors, synthesis, spreading):
    devices = lax.axis_size("gz")
    total_planes = PLANES * devices
    small, send_up, send_down = pack(moments, jnp.transpose(shapes, (1, 0, 2)), anchors.T)
    up = shifted(send_up, 1)
    down = shifted(send_down, -1)
    below2 = shifted(small, 2)
    above2 = shifted(small, -2)
    high, low = couple(jnp.pad(synthesis, ((0, 0), (0, LANES - COEFS))), spreading)

    rows, edge = tail_rows(0, 2, 1)[0], ANCHOR_LANE - 256
    places = jnp.concatenate(
        [
            below2[:, ANCHOR_LANE],
            up[rows, edge],
            small[:, ANCHOR_LANE],
            down[rows, edge],
            above2[:, ANCHOR_LANE],
        ]
    ).astype(jnp.int32)
    half = total_planes // 2
    local = (places - PLANES * lax.axis_index("gz") + half) % total_planes - half
    slots = jnp.where(jnp.arange(ROWS, dtype=jnp.int32) % GROUP < OWNED, local, places)

    rest = (small, below2, above2)
    for step in range(STEPS):
        last = step == STEPS - 1
        results = advance(step == 0, last, slots, high, low, moments, up, down, *rest)
        moments, sums = results[:2]
        if not last:
            state, send_up, send_down = results[2:5]
            if step == 0:
                order = results[5]
            up, down = shifted(send_up, 1), shifted(send_down, -1)
            rest = (state, sums, order)

    group = [sums[i * GROUP : (i + 1) * GROUP] for i in range(BLOCKS)]
    change = group[2] + shifted(group[3], 1) + shifted(group[1], -1) + shifted(group[0], -2)
    change = jnp.transpose(change.reshape(3, OWNED, LANES)[:, :, :COEFS], (1, 0, 2))
    return (moments, shapes + MOBILITY * change)


def solution(mesh):
    return jax.shard_map(
        per_device,
        mesh=mesh,
        in_specs=(P(None, "gz", None, None), P("gz", None, None), P("gz", None), P(), P()),
        out_specs=(P(None, "gz", None, None), P("gz", None, None)),
        check_vma=False,
    )
```

```python
import functools

import jax
import jax.numpy as jnp
from jax import lax
from jax.experimental import pallas as pl
from jax.experimental.pallas import tpu as pltpu
from jax.sharding import PartitionSpec as P


LMAX = 16
BZ = 8
BXY = 16
STEPS = 3
STIFF_SCALE = 0.002
MOBILITY = 0.5

PLANES = 8
SIDE = 128
OWNED = 8
COEFS = 289
SLOTS = 40
ORDER = 48
LANES = 384
KEPT = 304
CELLS = 2048
POINTS = 512
GROUP = OWNED * 3
BLOCKS = 5
ROWS = GROUP * BLOCKS
ANCHOR_LANE = 300
FIELDS = 10
SENT = 9 * SIDE
NARROW = COEFS - 256
STEP_LANES = 40
PADDED = 144
PITCH = 145
DEPTH = PLANES + 2 * BZ + 1
BOXED = ROWS + 1
CHUNK = 16
WIDE = 64
BATCH = 4
JK = ((0, 0), (1, 0), (2, 0), (0, 1), (1, 1), (0, 2))

VMEM = pl.BlockSpec(memory_space=pltpu.VMEM)
SMEM = pl.BlockSpec(memory_space=pltpu.SMEM)
HBM = pl.BlockSpec(memory_space=pltpu.HBM)
F32 = jnp.float32
BF16 = jnp.bfloat16


def shifted(block, distance):
    devices = lax.axis_size("gz")
    return lax.ppermute(block, "gz", [((i - distance) % devices, i) for i in range(devices)])


def split(value):
    high = value.astype(BF16)
    return high, (value - high.astype(F32)).astype(BF16)


def tail_rows(owner, part, owners):
    if part < 2:
        group, lane = owner * 2 + part, 0
    else:
        group, lane = owners * 2 + owner // 3, STEP_LANES * (owner % 3)
    start = SENT + group * GROUP
    return slice(start, start + GROUP), lane


def message_rows(owners):
    return SENT + (owners * 2 + (owners + 2) // 3) * GROUP


def read_tail(ref, owner, part, owners):
    rows, lane = tail_rows(owner, part, owners)
    value = ref[rows]
    if part == 2:
        if lane:
            value = pltpu.roll(value, 128 - lane, 1)
        lanes = lax.broadcasted_iota(jnp.int32, value.shape, 1)
        value = jnp.where(lanes < NARROW, value, 0.0)
    return value


def write_tail(ref, values, width):
    owners = values
    for owner in range(owners):
        for part in range(2):
            ref[tail_rows(owner, part, owners)[0]] = width(owner, part)
    for first in range(0, owners, 3):
        packed = width(first, 2)
        for owner in range(first + 1, min(first + 3, owners)):
            packed = packed + pltpu.roll(width(owner, 2), STEP_LANES * (owner - first), 1)
        ref[tail_rows(first, 2, owners)[0]] = packed


def write_plane(ref, field):
    trace = field(4)
    values = [field(0) - 0.6 * trace, field(1), field(2), field(3)]
    values += [field(5) - 0.2 * trace, field(6) - 0.2 * trace, field(7), field(8), field(9)]
    for n, value in enumerate(values):
        ref[n * SIDE : n * SIDE + SIDE] = value


def slot_row(slot):
    return slot + (slot // OWNED) * (2 * OWNED)


def chunk_row(n):
    return (n % 2 * 8 + n // 2) * BOXED


def couple_kernel(synthesis_ref, spreading_ref, high_ref, low_ref):
    width = 512
    turned = jnp.concatenate(split(synthesis_ref[...].T[0:KEPT]), axis=0)
    for ref in (high_ref, low_ref):
        ref[KEPT:] = jnp.zeros((LANES - KEPT, CELLS), BF16)
    for first in range(0, CELLS, width):
        lanes = slice(first, first + width)
        w_high, w_low = split(spreading_ref[:, lanes])
        main = jnp.dot(turned, w_high, preferred_element_type=F32)
        rest = jnp.dot(turned[0:KEPT], w_low, preferred_element_type=F32)
        high_ref[0:KEPT, lanes], low_ref[0:KEPT, lanes] = split(main[:KEPT] + (main[KEPT:] + rest))


def couple(synthesis, spreading):
    shape = jax.ShapeDtypeStruct((LANES, CELLS), BF16)
    return pl.pallas_call(
        couple_kernel,
        out_shape=(shape, shape),
        in_specs=[VMEM, VMEM],
        out_specs=[VMEM, VMEM],
        compiler_params=pltpu.CompilerParams(vmem_limit_bytes=32 * 2**20),
        cost_estimate=pl.CostEstimate(
            flops=6 * LANES * POINTS * CELLS, bytes_accessed=8 * 2**20, transcendentals=0
        ),
        name="couple",
    )(synthesis, spreading)


def pack_kernel(anchors_ref, moments_hbm, shapes_ref, small_ref, up_ref, down_ref, planes, sem):
    copies = [
        pltpu.make_async_copy(moments_hbm.at[:, z], planes.at[n], sem.at[n])
        for n, z in enumerate((PLANES - 1, 0))
    ]
    for copy in copies:
        copy.start()
    small_ref[...] = jnp.zeros_like(small_ref)
    for c in range(3):
        small_ref[c * OWNED : c * OWNED + OWNED, 0:COEFS] = shapes_ref[c]
    part = small_ref[:, 256:LANES]
    row = lax.broadcasted_iota(jnp.int32, part.shape, 0)
    anchor = jnp.zeros(part.shape, jnp.int32)
    for n in range(GROUP):
        anchor = jnp.where(row == n, anchors_ref[n // OWNED, n % OWNED], anchor)
    lane = lax.broadcasted_iota(jnp.int32, part.shape, 1)
    part = jnp.where(lane == ANCHOR_LANE - 256, anchor.astype(F32), part)
    small_ref[:, 256:LANES] = part
    for ref in (up_ref, down_ref):
        write_tail(ref, 1, lambda owner, p: small_ref[:, p * 128 : p * 128 + 128])
    for n, ref in enumerate((up_ref, down_ref)):
        copies[n].wait()
        write_plane(ref, lambda f, n=n: planes[n, f])


def pack(moments, shapes, anchors):
    shape = jax.ShapeDtypeStruct((message_rows(1), SIDE), F32)
    return pl.pallas_call(
        pack_kernel,
        out_shape=(jax.ShapeDtypeStruct((GROUP, LANES), F32), shape, shape),
        in_specs=[SMEM, HBM, VMEM],
        out_specs=[VMEM, VMEM, VMEM],
        scratch_shapes=[pltpu.VMEM((2, FIELDS, SIDE, SIDE), F32), pltpu.SemaphoreType.DMA((2,))],
        compiler_params=pltpu.CompilerParams(vmem_limit_bytes=60 * 2**20),
        name="pack",
    )(anchors, moments, shapes)


def spread_x(zero, one, two):
    plus = zero if two is None else zero + two
    minus = plus
    if one is not None:
        plus, minus = plus + one, plus - one
    plus = pltpu.roll(plus, 1, 1)
    minus = pltpu.roll(minus, SIDE - 1, 1)
    both = plus + minus
    return (4.0 * zero + both, plus - minus, both)


def collide_rows(m, force):
    unit = 1.0 / 216.0
    rho = m[0]
    u = [m[1 + a] + 0.5 * force[a] for a in range(3)]
    t = [0.625 * u[a] + 0.375 * force[a] for a in range(3)]
    v = [(9.0 * unit) * u[a] for a in range(3)]
    line = [(3.0 * unit) * (m[1 + a] + force[a]) for a in range(3)]
    shared = (0.375 * unit) * rho
    square = [shared - (1.125 * unit) * m[4 + a] + v[a] * t[a] for a in range(3)]
    cross = [
        v[a] * t[b] + v[b] * t[a] - (2.25 * unit) * m[7 + n]
        for n, (a, b) in enumerate(((0, 1), (0, 2), (1, 2)))
    ]
    cell = unit * rho - (1.0 / 3.0) * (square[0] + square[1] + square[2])
    return cell, line, square, cross


def step_kernel(first, last, *refs):
    refs = list(refs)

    def take(count):
        taken = refs[:count]
        del refs[:count]
        return taken

    slots_ref, high_ref, low_ref, moments_hbm, up_ref, down_ref = take(6)
    if first:
        own_ref, below_ref, above_ref = take(3)
    else:
        state_ref, sum_ref, order_ref = take(3)
    out_hbm, newsum_ref = take(2)
    if not last:
        newstate_ref, sendup_ref, senddown_ref = take(3)
    if first:
        (order_ref,) = take(1)
    (
        old, new, velocity, force, boxes, sampled,
        shifts, stills, ring, middle, state,
        in_sem, out_sem,
    ) = refs

    for z in range(PLANES):
        pltpu.make_async_copy(moments_hbm.at[:, z], old.at[:, z + 1], in_sem.at[z]).start()

    if first:

        def scan(slot, carry):
            count, spare = carry
            above = slots_ref[slot_row(slot)]
            near = jnp.logical_and(above >= -BZ, above <= PLANES)

            @pl.when(near)
            def _():
                order_ref[count] = slot

            return count + near.astype(jnp.int32), jnp.where(near, spare, slot)

        count, spare = lax.fori_loop(0, SLOTS, scan, (jnp.int32(0), jnp.int32(0)))
        for n in range(BATCH - 1):
            order_ref[count + n] = spare
        order_ref[ORDER - 1] = (count + BATCH - 1) // BATCH
    rounds = order_ref[ORDER - 1]

    for c in range(3):
        start = (c * DEPTH + BZ - 1) * PITCH
        force[start : start + (PLANES + 2) * PITCH] = jnp.zeros(((PLANES + 2) * PITCH, SIDE), F32)
    sampled[...] = jnp.zeros_like(sampled)
    for ref, edge in ((up_ref, 0), (down_ref, PLANES + 1)):
        for n, f in enumerate((0, 1, 2, 3, 5, 6, 7, 8, 9)):
            old[f, edge] = ref[n * SIDE : n * SIDE + SIDE]
        old[4, edge] = jnp.zeros((SIDE, SIDE), F32)

    for part in range(3):
        lanes = slice(part * 128, part * 128 + 128)
        for owner in range(BLOCKS):
            rows = slice(owner * GROUP, owner * GROUP + GROUP)
            if first:
                if owner % 2 == 1:
                    value = read_tail(up_ref if owner == 1 else down_ref, 0, part, 1)
                else:
                    value = (below_ref, own_ref, above_ref)[owner // 2][:, lanes]
                    if part == 2:
                        lane = lax.broadcasted_iota(jnp.int32, value.shape, 1)
                        value = jnp.where(lane < NARROW, value, 0.0)
            else:
                value = state_ref[rows, lanes]
                if owner < 3:
                    value = value + MOBILITY * read_tail(up_ref, owner, part, 3)
                if owner > 0:
                    value = value + MOBILITY * read_tail(down_ref, owner - 1, part, 4)
            state[rows, lanes] = value

    number = lax.broadcasted_iota(jnp.int32, (1, LANES), 1)
    degree = jnp.zeros((1, LANES), jnp.int32)
    for step in range(1, LMAX + 1):
        degree = degree + (number >= step * step).astype(jnp.int32)
    stiffness = STIFF_SCALE * (degree * (degree + 1) + 2).astype(F32)
    coef_high, coef_low = split(-stiffness * state[...])
    both = jnp.concatenate([coef_high, coef_low], axis=0)
    for part in range(CELLS // 512):
        lanes = slice(part * 512, part * 512 + 512)
        main = jnp.dot(both, high_ref[:, lanes], preferred_element_type=F32)
        rest = jnp.dot(coef_high, low_ref[:, lanes], preferred_element_type=F32)
        whole = main[:ROWS] + (main[ROWS:] + rest)
        for chunk in range(4):
            start = chunk_row(part * 4 + chunk)
            boxes[start : start + ROWS] = whole[:, chunk * 128 : chunk * 128 + 128]

    def box_parts(slot):
        base = slot_row(slot)
        above = slots_ref[base]
        near = jnp.logical_and(above >= -BZ, above <= PLANES)
        above = jnp.where(near, above, PLANES + 1)
        row = slots_ref[base + OWNED]
        column = slots_ref[base + 2 * OWNED]
        lane = lax.broadcasted_iota(jnp.int32, (BXY, SIDE), 1)
        inside = lax.broadcasted_iota(jnp.int32, (BXY, SIDE), 0)
        hit = (((lane - column) & (SIDE - 1)) == inside).astype(F32).astype(BF16)
        none = jnp.zeros((BXY, SIDE), BF16)
        spots = jnp.concatenate(
            [jnp.concatenate([hit if i == n else none for i in range(8)], axis=1) for n in range(8)],
            axis=0,
        )
        starts = [
            (c * DEPTH + above + BZ) * PITCH + row + half * 8 for c in range(3) for half in range(2)
        ]
        rows = [half * 8 * BOXED + base + c * OWNED for c in range(3) for half in range(2)]
        return above, spots, starts, rows

    def place_batch(batch, carry):
        found = []
        for n in range(BATCH):
            _, spots, starts, rows = box_parts(order_ref[batch * BATCH + n])
            cells = jnp.concatenate([boxes[pl.ds(start, 8, stride=BOXED)] for start in rows], axis=0)
            placed = jnp.dot(
                jnp.concatenate(split(cells), axis=1),
                jnp.concatenate([spots, spots], axis=0),
                preferred_element_type=F32,
            )
            found.append((starts, placed))
        for starts, placed in found:
            where = [
                (pl.ds(start + i, 8, stride=PITCH), slice(n * 8, n * 8 + 8), slice(i * 128, i * 128 + 128))
                for n, start in enumerate(starts)
                for i in range(8)
            ]
            sums = [force[there] + placed[here, lanes] for there, here, lanes in where]
            for (there, here, lanes), value in zip(where, sums):
                force[there] = value
        return carry

    lax.fori_loop(0, rounds, place_batch, 0)

    def fold(z, carry):
        for c in range(3):
            start = (c * DEPTH + z + BZ - 1) * PITCH
            first = pl.ds(start, BXY)
            force[first] = force[first] + force[pl.ds(start + SIDE, BXY)]
        return carry

    lax.fori_loop(0, PLANES + 2, fold, 0)

    def stream_plane(z, carry):
        @pl.when(jnp.logical_and(z >= 1, z <= PLANES))
        def _():
            pltpu.make_async_copy(moments_hbm.at[:, 0], old.at[:, z], in_sem.at[z - 1]).wait()


        def collide_chunk(step, carry):
            y = pl.multiple_of(step * WIDE, WIDE)
            rows = pl.ds(y, WIDE)
            m = [old[f, z, rows] for f in range(FIELDS)]
            cell, line, square, cross = collide_rows(
                m, [force[pl.ds((c * DEPTH + z + BZ - 1) * PITCH + y, WIDE)] for c in range(3)]
            )
            even = [
                spread_x(cell, line[2], square[2]),
                spread_x(line[1], cross[2], None),
                spread_x(square[1], None, None),
            ]
            twice = spread_x(square[0], None, None)
            odd = [spread_x(line[0], cross[1], None), spread_x(cross[0], None, None)]
            moved = pl.ds(y + 8, WIDE)
            for k in range(3):
                ends = even[0][k] + even[2][k]
                shifts[k, moved] = ends + even[1][k]
                shifts[3 + k, moved] = ends - even[1][k]
                shifts[6 + k, moved] = odd[0][k] + odd[1][k]
                shifts[9 + k, moved] = odd[0][k] - odd[1][k]
                shifts[12 + k, moved] = twice[k]
                stills[k, rows] = 4.0 * even[0][k]
                stills[3 + k, rows] = 4.0 * odd[0][k]
            return carry

        lax.fori_loop(0, SIDE // WIDE, collide_chunk, 0)
        for field in range(15):
            shifts[field, 7:8] = shifts[field, SIDE + 7 : SIDE + 8]
            shifts[field, SIDE + 8 : SIDE + 9] = shifts[field, 8:9]
        parity = z % 2
        inner = jnp.clip(z - 2, 0, PLANES - 1)

        for step in range(SIDE // CHUNK):
            y = step * CHUNK
            rows = slice(y, y + CHUNK)
            after = slice(y + 7, y + 7 + CHUNK)
            before = slice(y + 9, y + 9 + CHUNK)
            even, odd, twice = {}, {}, {}
            for k in range(3):
                for target, plus, minus, still in (
                    (even, k, 3 + k, lambda k=k: stills[k, rows]),
                    (odd, 6 + k, 9 + k, lambda k=k: stills[3 + k, rows]),
                    (twice, 12 + k, 12 + k, lambda k=k: 4.0 * shifts[12 + k, y + 8 : y + 8 + CHUNK]),
                ):
                    up, down = shifts[plus, after], shifts[minus, before]
                    both = up + down
                    target[0, k] = still() + both
                    if k < 2:
                        target[1, k] = up - down
                    if k < 1:
                        target[2, k] = both
            total, difference, centre = {}, {}, {}
            for n, key in enumerate(JK):
                ends = even[key] + twice[key]
                under = ring[parity, n, rows]
                over = ends - odd[key]
                total[key] = under + over
                difference[key] = under - over
                centre[key] = middle[n, rows] + total[key]
                ring[parity, n, rows] = ends + odd[key]
                middle[n, rows] = 4.0 * even[key]
            flow = (difference[0, 0], centre[1, 0], centre[0, 1])
            results = (
                centre[0, 0], *flow, total[0, 0], centre[2, 0], centre[0, 2],
                difference[1, 0], difference[0, 1], centre[1, 1],
            )
            for f, value in enumerate(results):
                new[f, z, rows] = value
            for c in range(3):
                start = (c * DEPTH + inner + BZ) * PITCH
                velocity[pl.ds(start + y, CHUNK)] = flow[c]
                if step == 0:
                    velocity[pl.ds(start + SIDE, BXY)] = flow[c]

        @pl.when(z >= 2)
        def _():
            pltpu.make_async_copy(new.at[:, z], out_hbm.at[:, z - 2], out_sem.at[z - 2]).start()

        return carry

    lax.fori_loop(0, PLANES + 2, stream_plane, 0)

    if not last:
        write_plane(sendup_ref, lambda f: new[f, PLANES + 1])
        write_plane(senddown_ref, lambda f: new[f, 2])

    across = functools.partial(
        lax.dot_general, dimension_numbers=(((1,), (1,)), ((), ())), preferred_element_type=F32
    )

    def sample_batch(batch, carry):
        results = []
        for n in range(BATCH):
            above, spots, starts, rows = box_parts(order_ref[batch * BATCH + n])
            cells = jnp.concatenate(
                [
                    jnp.concatenate([velocity[pl.ds(start + i, 8, stride=PITCH)] for i in range(8)], axis=1)
                    for start in starts
                ],
                axis=0,
            )
            results.append((above, rows, across(jnp.concatenate(split(cells), axis=0), spots)))
        for above, rows, found in results:
            plane = lax.broadcasted_iota(jnp.int32, (8, SIDE), 0) + above
            ours = jnp.logical_and(plane >= 0, plane < PLANES)
            for n, start in enumerate(rows):
                value = found[n * 8 : n * 8 + 8] + found[48 + n * 8 : 56 + n * 8]
                sampled[pl.ds(start, 8, stride=BOXED)] = jnp.where(ours, value, 0.0)
        return carry

    lax.fori_loop(0, rounds, sample_batch, 0)

    part_high, part_low = split(
        jnp.concatenate([sampled[chunk_row(n) : chunk_row(n) + ROWS] for n in range(16)], axis=1)
    )
    main = across(jnp.concatenate([part_high, part_low], axis=0), high_ref[...])
    partial = main[:ROWS] + (main[ROWS:] + across(part_high, low_ref[...]))

    newsum_ref[...] = partial if first else sum_ref[...] + partial
    if not last:
        newstate_ref[...] = state[...] + MOBILITY * partial
        for ref, start, owners in ((sendup_ref, GROUP, 3), (senddown_ref, 0, 4)):
            write_tail(
                ref,
                owners,
                lambda owner, part: partial[
                    start + owner * GROUP : start + owner * GROUP + GROUP, part * 128 : part * 128 + 128
                ],
            )
    for z in range(PLANES):
        pltpu.make_async_copy(new.at[:, z + 2], out_hbm.at[:, z], out_sem.at[z]).wait()


def advance(first, last, slots, high, low, moments, up, down, *rest):
    square = (SIDE, SIDE)
    out_shape = [
        jax.ShapeDtypeStruct((FIELDS, PLANES) + square, F32),
        jax.ShapeDtypeStruct((ROWS, LANES), F32),
    ]
    out_specs = [HBM, VMEM]
    if not last:
        out_shape += [
            jax.ShapeDtypeStruct((ROWS, LANES), F32),
            jax.ShapeDtypeStruct((message_rows(3), SIDE), F32),
            jax.ShapeDtypeStruct((message_rows(4), SIDE), F32),
        ]
        out_specs += [VMEM] * 3
    if first:
        out_shape.append(jax.ShapeDtypeStruct((ORDER,), jnp.int32))
        out_specs.append(SMEM)
    scratch = [
        pltpu.VMEM((FIELDS, PLANES + 2) + square, F32),
        pltpu.VMEM((FIELDS, PLANES + 2) + square, F32),
        pltpu.VMEM((3 * DEPTH * PITCH, SIDE), F32),
        pltpu.VMEM((3 * DEPTH * PITCH, SIDE), F32),
        pltpu.VMEM((CELLS // 128 * BOXED, 128), F32),
        pltpu.VMEM((CELLS // 128 * BOXED, 128), F32),
        pltpu.VMEM((15, PADDED, SIDE), F32),
        pltpu.VMEM((6,) + square, F32),
        pltpu.VMEM((2, 6) + square, F32),
        pltpu.VMEM((6,) + square, F32),
        pltpu.VMEM((ROWS, LANES), F32),
        pltpu.SemaphoreType.DMA((PLANES,)),
        pltpu.SemaphoreType.DMA((PLANES,)),
    ]
    return pl.pallas_call(
        functools.partial(step_kernel, first, last),
        out_shape=out_shape,
        in_specs=[SMEM, VMEM, VMEM, HBM, VMEM, VMEM] + [VMEM] * 2 + [VMEM if first else SMEM],
        out_specs=out_specs,
        scratch_shapes=scratch,
        compiler_params=pltpu.CompilerParams(vmem_limit_bytes=44 * 2**20),
        cost_estimate=pl.CostEstimate(
            flops=4 * 10**8, bytes_accessed=16 * 2**20, transcendentals=0
        ),
        input_output_aliases={} if first else {3: 0},
        name="first_step" if first else "last_step" if last else "step",
    )(slots, high, low, moments, up, down, *rest)


def per_device(moments, shapes, anchors, synthesis, spreading):
    devices = lax.axis_size("gz")
    total_planes = PLANES * devices
    small, send_up, send_down = pack(moments, jnp.transpose(shapes, (1, 0, 2)), anchors.T)
    up = shifted(send_up, 1)
    down = shifted(send_down, -1)
    below2 = shifted(small, 2)
    above2 = shifted(small, -2)
    high, low = couple(jnp.pad(synthesis, ((0, 0), (0, LANES - COEFS))), spreading)

    rows, edge = tail_rows(0, 2, 1)[0], ANCHOR_LANE - 256
    places = jnp.concatenate(
        [
            below2[:, ANCHOR_LANE],
            up[rows, edge],
            small[:, ANCHOR_LANE],
            down[rows, edge],
            above2[:, ANCHOR_LANE],
        ]
    ).astype(jnp.int32)
    half = total_planes // 2
    local = (places - PLANES * lax.axis_index("gz") + half) % total_planes - half
    slots = jnp.where(jnp.arange(ROWS, dtype=jnp.int32) % GROUP < OWNED, local, places)

    rest = (small, below2, above2)
    for step in range(STEPS):
        last = step == STEPS - 1
        results = advance(step == 0, last, slots, high, low, moments, up, down, *rest)
        moments, sums = results[:2]
        if not last:
            state, send_up, send_down = results[2:5]
            if step == 0:
                order = results[5]
            up, down = shifted(send_up, 1), shifted(send_down, -1)
            rest = (state, sums, order)

    group = [sums[i * GROUP : (i + 1) * GROUP] for i in range(BLOCKS)]
    change = group[2] + shifted(group[3], 1) + shifted(group[1], -1) + shifted(group[0], -2)
    change = jnp.transpose(change.reshape(3, OWNED, LANES)[:, :, :COEFS], (1, 0, 2))
    return (moments, shapes + MOBILITY * change)


def solution(mesh):
    return jax.shard_map(
        per_device,
        mesh=mesh,
        in_specs=(P(None, "gz", None, None), P("gz", None, None), P("gz", None), P(), P()),
        out_specs=(P(None, "gz", None, None), P("gz", None, None)),
        check_vma=False,
    )
```

```python
import functools

import jax
import jax.numpy as jnp
from jax import lax
from jax.experimental import pallas as pl
from jax.experimental.pallas import tpu as pltpu
from jax.sharding import PartitionSpec as P


LMAX = 16
BZ = 8
BXY = 16
STEPS = 3
STIFF_SCALE = 0.002
MOBILITY = 0.5

PLANES = 8
SIDE = 128
OWNED = 8
COEFS = 289
SLOTS = 40
ORDER = 48
LANES = 384
KEPT = 304
CELLS = 2048
POINTS = 512
GROUP = OWNED * 3
BLOCKS = 5
ROWS = GROUP * BLOCKS
ANCHOR_LANE = 300
FIELDS = 10
SENT = 9 * SIDE
NARROW = COEFS - 256
STEP_LANES = 40
PADDED = 144
PITCH = 145
DEPTH = PLANES + 2 * BZ + 1
BOXED = ROWS + 1
CHUNK = 16
WIDE = 16
UNROLL = 8
BATCH = 4
JK = ((0, 0), (1, 0), (2, 0), (0, 1), (1, 1), (0, 2))

VMEM = pl.BlockSpec(memory_space=pltpu.VMEM)
SMEM = pl.BlockSpec(memory_space=pltpu.SMEM)
HBM = pl.BlockSpec(memory_space=pltpu.HBM)
F32 = jnp.float32
BF16 = jnp.bfloat16


def shifted(block, distance):
    devices = lax.axis_size("gz")
    return lax.ppermute(block, "gz", [((i - distance) % devices, i) for i in range(devices)])


def split(value):
    high = value.astype(BF16)
    return high, (value - high.astype(F32)).astype(BF16)


def tail_rows(owner, part, owners):
    if part < 2:
        group, lane = owner * 2 + part, 0
    else:
        group, lane = owners * 2 + owner // 3, STEP_LANES * (owner % 3)
    start = SENT + group * GROUP
    return slice(start, start + GROUP), lane


def message_rows(owners):
    return SENT + (owners * 2 + (owners + 2) // 3) * GROUP


def read_tail(ref, owner, part, owners):
    rows, lane = tail_rows(owner, part, owners)
    value = ref[rows]
    if part == 2:
        if lane:
            value = pltpu.roll(value, 128 - lane, 1)
        lanes = lax.broadcasted_iota(jnp.int32, value.shape, 1)
        value = jnp.where(lanes < NARROW, value, 0.0)
    return value


def write_tail(ref, values, width):
    owners = values
    for owner in range(owners):
        for part in range(2):
            ref[tail_rows(owner, part, owners)[0]] = width(owner, part)
    for first in range(0, owners, 3):
        packed = width(first, 2)
        for owner in range(first + 1, min(first + 3, owners)):
            packed = packed + pltpu.roll(width(owner, 2), STEP_LANES * (owner - first), 1)
        ref[tail_rows(first, 2, owners)[0]] = packed


def write_plane(ref, field):
    trace = field(4)
    values = [field(0) - 0.6 * trace, field(1), field(2), field(3)]
    values += [field(5) - 0.2 * trace, field(6) - 0.2 * trace, field(7), field(8), field(9)]
    for n, value in enumerate(values):
        ref[n * SIDE : n * SIDE + SIDE] = value


def slot_row(slot):
    return slot + (slot // OWNED) * (2 * OWNED)


def chunk_row(n):
    return (n % 2 * 8 + n // 2) * BOXED


def couple_kernel(synthesis_ref, spreading_ref, high_ref, low_ref):
    width = 512
    turned = jnp.concatenate(split(synthesis_ref[...].T[0:KEPT]), axis=0)
    for ref in (high_ref, low_ref):
        ref[KEPT:] = jnp.zeros((LANES - KEPT, CELLS), BF16)
    for first in range(0, CELLS, width):
        lanes = slice(first, first + width)
        w_high, w_low = split(spreading_ref[:, lanes])
        main = jnp.dot(turned, w_high, preferred_element_type=F32)
        rest = jnp.dot(turned[0:KEPT], w_low, preferred_element_type=F32)
        high_ref[0:KEPT, lanes], low_ref[0:KEPT, lanes] = split(main[:KEPT] + (main[KEPT:] + rest))


def couple(synthesis, spreading):
    shape = jax.ShapeDtypeStruct((LANES, CELLS), BF16)
    return pl.pallas_call(
        couple_kernel,
        out_shape=(shape, shape),
        in_specs=[VMEM, VMEM],
        out_specs=[VMEM, VMEM],
        compiler_params=pltpu.CompilerParams(vmem_limit_bytes=32 * 2**20),
        cost_estimate=pl.CostEstimate(
            flops=6 * LANES * POINTS * CELLS, bytes_accessed=8 * 2**20, transcendentals=0
        ),
        name="couple",
    )(synthesis, spreading)


def pack_kernel(anchors_ref, moments_hbm, shapes_ref, small_ref, up_ref, down_ref, planes, sem):
    copies = [
        pltpu.make_async_copy(moments_hbm.at[:, z], planes.at[n], sem.at[n])
        for n, z in enumerate((PLANES - 1, 0))
    ]
    for copy in copies:
        copy.start()
    small_ref[...] = jnp.zeros_like(small_ref)
    for c in range(3):
        small_ref[c * OWNED : c * OWNED + OWNED, 0:COEFS] = shapes_ref[c]
    part = small_ref[:, 256:LANES]
    row = lax.broadcasted_iota(jnp.int32, part.shape, 0)
    anchor = jnp.zeros(part.shape, jnp.int32)
    for n in range(GROUP):
        anchor = jnp.where(row == n, anchors_ref[n // OWNED, n % OWNED], anchor)
    lane = lax.broadcasted_iota(jnp.int32, part.shape, 1)
    part = jnp.where(lane == ANCHOR_LANE - 256, anchor.astype(F32), part)
    small_ref[:, 256:LANES] = part
    for ref in (up_ref, down_ref):
        write_tail(ref, 1, lambda owner, p: small_ref[:, p * 128 : p * 128 + 128])
    for n, ref in enumerate((up_ref, down_ref)):
        copies[n].wait()
        write_plane(ref, lambda f, n=n: planes[n, f])


def pack(moments, shapes, anchors):
    shape = jax.ShapeDtypeStruct((message_rows(1), SIDE), F32)
    return pl.pallas_call(
        pack_kernel,
        out_shape=(jax.ShapeDtypeStruct((GROUP, LANES), F32), shape, shape),
        in_specs=[SMEM, HBM, VMEM],
        out_specs=[VMEM, VMEM, VMEM],
        scratch_shapes=[pltpu.VMEM((2, FIELDS, SIDE, SIDE), F32), pltpu.SemaphoreType.DMA((2,))],
        compiler_params=pltpu.CompilerParams(vmem_limit_bytes=60 * 2**20),
        name="pack",
    )(anchors, moments, shapes)


def spread_x(zero, one, two):
    plus = zero if two is None else zero + two
    minus = plus
    if one is not None:
        plus, minus = plus + one, plus - one
    plus = pltpu.roll(plus, 1, 1)
    minus = pltpu.roll(minus, SIDE - 1, 1)
    both = plus + minus
    return (4.0 * zero + both, plus - minus, both)


def collide_rows(m, force):
    unit = 1.0 / 216.0
    rho = m[0]
    u = [m[1 + a] + 0.5 * force[a] for a in range(3)]
    t = [0.625 * u[a] + 0.375 * force[a] for a in range(3)]
    v = [(9.0 * unit) * u[a] for a in range(3)]
    line = [(3.0 * unit) * (m[1 + a] + force[a]) for a in range(3)]
    shared = (0.375 * unit) * rho
    square = [shared - (1.125 * unit) * m[4 + a] + v[a] * t[a] for a in range(3)]
    cross = [
        v[a] * t[b] + v[b] * t[a] - (2.25 * unit) * m[7 + n]
        for n, (a, b) in enumerate(((0, 1), (0, 2), (1, 2)))
    ]
    cell = unit * rho - (1.0 / 3.0) * (square[0] + square[1] + square[2])
    return cell, line, square, cross


def step_kernel(first, last, total_planes, *refs):
    refs = list(refs)

    def take(count):
        taken = refs[:count]
        del refs[:count]
        return taken

    slots_ref, high_ref, low_ref, moments_hbm, up_ref, down_ref = take(6)
    if first:
        own_ref, below_ref, above_ref = take(3)
    else:
        state_ref, sum_ref, order_ref = take(3)
    out_hbm, newsum_ref = take(2)
    if not last:
        newstate_ref, sendup_ref, senddown_ref = take(3)
    if first:
        order_ref, places_ref = take(2)
    (
        old, new, velocity, force, boxes, sampled,
        shifts, stills, ring, middle, state,
        in_sem, out_sem, slot_sem, slots_smem,
    ) = refs

    for z in range(PLANES):
        pltpu.make_async_copy(moments_hbm.at[:, z], old.at[:, z + 1], in_sem.at[z]).start()

    if first:
        home_ref, slots_ref = slots_ref, slots_smem
        row = lax.broadcasted_iota(jnp.int32, (GROUP, 128), 0)
        lane = lax.broadcasted_iota(jnp.int32, (GROUP, 128), 1)
        last_part = tail_rows(0, 2, 1)[0]
        values = (
            below_ref[:, 256:LANES], up_ref[last_part], own_ref[:, 256:LANES],
            down_ref[last_part], above_ref[:, 256:LANES],
        )
        edge = ANCHOR_LANE - 256
        spots = jnp.zeros((GROUP, 128), F32)
        for owner, value in enumerate(values):
            column = jnp.broadcast_to(value[:, edge : edge + 1], (GROUP, 128))
            spots = jnp.where(lane == row + owner * GROUP, column, spots)
        spots = jnp.sum(spots, axis=0, keepdims=True).astype(jnp.int32)
        lane = lane[0:1]
        along = functools.reduce(
            jnp.logical_or,
            [
                jnp.logical_and(lane >= owner * GROUP, lane < owner * GROUP + OWNED)
                for owner in range(BLOCKS)
            ],
        )
        half = total_planes // 2
        local = ((spots - home_ref[0] + half) & (total_planes - 1)) - half
        places_ref[...] = jnp.where(along, local, spots)
        copy = pltpu.make_async_copy(places_ref, slots_smem, slot_sem.at[0])
        copy.start()
        copy.wait()

    if first:

        def scan(slot, carry):
            count, spare = carry
            above = slots_ref[0, slot_row(slot)]
            near = jnp.logical_and(above >= -BZ, above <= PLANES)

            @pl.when(near)
            def _():
                order_ref[count] = slot

            return count + near.astype(jnp.int32), jnp.where(near, spare, slot)

        count, spare = lax.fori_loop(0, SLOTS, scan, (jnp.int32(0), jnp.int32(0)))
        for n in range(BATCH - 1):
            order_ref[count + n] = spare
        order_ref[ORDER - 1] = (count + BATCH - 1) // BATCH
    rounds = order_ref[ORDER - 1]

    for c in range(3):
        start = (c * DEPTH + BZ - 1) * PITCH
        force[start : start + (PLANES + 2) * PITCH] = jnp.zeros(((PLANES + 2) * PITCH, SIDE), F32)
    sampled[...] = jnp.zeros_like(sampled)
    for ref, edge in ((up_ref, 0), (down_ref, PLANES + 1)):
        for n, f in enumerate((0, 1, 2, 3, 5, 6, 7, 8, 9)):
            old[f, edge] = ref[n * SIDE : n * SIDE + SIDE]
        old[4, edge] = jnp.zeros((SIDE, SIDE), F32)

    for part in range(3):
        lanes = slice(part * 128, part * 128 + 128)
        for owner in range(BLOCKS):
            rows = slice(owner * GROUP, owner * GROUP + GROUP)
            if first:
                if owner % 2 == 1:
                    value = read_tail(up_ref if owner == 1 else down_ref, 0, part, 1)
                else:
                    value = (below_ref, own_ref, above_ref)[owner // 2][:, lanes]
                    if part == 2:
                        lane = lax.broadcasted_iota(jnp.int32, value.shape, 1)
                        value = jnp.where(lane < NARROW, value, 0.0)
            else:
                value = state_ref[rows, lanes]
                if owner < 3:
                    value = value + MOBILITY * read_tail(up_ref, owner, part, 3)
                if owner > 0:
                    value = value + MOBILITY * read_tail(down_ref, owner - 1, part, 4)
            state[rows, lanes] = value

    number = lax.broadcasted_iota(jnp.int32, (1, LANES), 1)
    degree = jnp.zeros((1, LANES), jnp.int32)
    for step in range(1, LMAX + 1):
        degree = degree + (number >= step * step).astype(jnp.int32)
    stiffness = STIFF_SCALE * (degree * (degree + 1) + 2).astype(F32)
    coef_high, coef_low = split(-stiffness * state[...])
    both = jnp.concatenate([coef_high, coef_low], axis=0)
    for part in range(CELLS // 512):
        lanes = slice(part * 512, part * 512 + 512)
        main = jnp.dot(both, high_ref[:, lanes], preferred_element_type=F32)
        rest = jnp.dot(coef_high, low_ref[:, lanes], preferred_element_type=F32)
        whole = main[:ROWS] + (main[ROWS:] + rest)
        for chunk in range(4):
            start = chunk_row(part * 4 + chunk)
            boxes[start : start + ROWS] = whole[:, chunk * 128 : chunk * 128 + 128]

    def box_parts(slot):
        base = slot_row(slot)
        above = slots_ref[0, base]
        near = jnp.logical_and(above >= -BZ, above <= PLANES)
        above = jnp.where(near, above, PLANES + 1)
        row = slots_ref[0, base + OWNED]
        column = slots_ref[0, base + 2 * OWNED]
        lane = lax.broadcasted_iota(jnp.int32, (BXY, SIDE), 1)
        inside = lax.broadcasted_iota(jnp.int32, (BXY, SIDE), 0)
        hit = (((lane - column) & (SIDE - 1)) == inside).astype(F32).astype(BF16)
        none = jnp.zeros((BXY, SIDE), BF16)
        spots = jnp.concatenate(
            [jnp.concatenate([hit if i == n else none for i in range(8)], axis=1) for n in range(8)],
            axis=0,
        )
        starts = [
            (c * DEPTH + above + BZ) * PITCH + row + half * 8 for c in range(3) for half in range(2)
        ]
        rows = [half * 8 * BOXED + base + c * OWNED for c in range(3) for half in range(2)]
        return above, spots, starts, rows

    def place_batch(batch, carry):
        found = []
        for n in range(BATCH):
            _, spots, starts, rows = box_parts(order_ref[batch * BATCH + n])
            cells = jnp.concatenate([boxes[pl.ds(start, 8, stride=BOXED)] for start in rows], axis=0)
            placed = jnp.dot(
                jnp.concatenate(split(cells), axis=1),
                jnp.concatenate([spots, spots], axis=0),
                preferred_element_type=F32,
            )
            found.append((starts, placed))
        for starts, placed in found:
            where = [
                (pl.ds(start + i, 8, stride=PITCH), slice(n * 8, n * 8 + 8), slice(i * 128, i * 128 + 128))
                for n, start in enumerate(starts)
                for i in range(8)
            ]
            sums = [force[there] + placed[here, lanes] for there, here, lanes in where]
            for (there, here, lanes), value in zip(where, sums):
                force[there] = value
        return carry

    lax.fori_loop(0, rounds, place_batch, 0)

    def fold(z, carry):
        for c in range(3):
            start = (c * DEPTH + z + BZ - 1) * PITCH
            first = pl.ds(start, BXY)
            force[first] = force[first] + force[pl.ds(start + SIDE, BXY)]
        return carry

    lax.fori_loop(0, PLANES + 2, fold, 0)

    def stream_plane(z, carry):
        @pl.when(jnp.logical_and(z >= 1, z <= PLANES))
        def _():
            pltpu.make_async_copy(moments_hbm.at[:, 0], old.at[:, z], in_sem.at[z - 1]).wait()


        def collide_chunk(y):
            rows = pl.ds(y, WIDE)
            m = [old[f, z, rows] for f in range(FIELDS)]
            cell, line, square, cross = collide_rows(
                m, [force[pl.ds((c * DEPTH + z + BZ - 1) * PITCH + y, WIDE)] for c in range(3)]
            )
            even = [
                spread_x(cell, line[2], square[2]),
                spread_x(line[1], cross[2], None),
                spread_x(square[1], None, None),
            ]
            twice = spread_x(square[0], None, None)
            odd = [spread_x(line[0], cross[1], None), spread_x(cross[0], None, None)]
            moved = pl.ds(y + 8, WIDE)
            for k in range(3):
                ends = even[0][k] + even[2][k]
                shifts[k, moved] = ends + even[1][k]
                shifts[3 + k, moved] = ends - even[1][k]
                shifts[6 + k, moved] = odd[0][k] + odd[1][k]
                shifts[9 + k, moved] = odd[0][k] - odd[1][k]
                shifts[12 + k, moved] = twice[k]
                stills[k, rows] = 4.0 * even[0][k]
                stills[3 + k, rows] = 4.0 * odd[0][k]

        def collide_some(step, carry):
            for n in range(UNROLL):
                collide_chunk(pl.multiple_of(step * (WIDE * UNROLL), WIDE * UNROLL) + n * WIDE)
            return carry

        lax.fori_loop(0, SIDE // (WIDE * UNROLL), collide_some, 0)
        for field in range(15):
            shifts[field, 7:8] = shifts[field, SIDE + 7 : SIDE + 8]
            shifts[field, SIDE + 8 : SIDE + 9] = shifts[field, 8:9]
        parity = z % 2
        inner = jnp.clip(z - 2, 0, PLANES - 1)

        for step in range(SIDE // CHUNK):
            y = step * CHUNK
            rows = slice(y, y + CHUNK)
            after = slice(y + 7, y + 7 + CHUNK)
            before = slice(y + 9, y + 9 + CHUNK)
            even, odd, twice = {}, {}, {}
            for k in range(3):
                for target, plus, minus, still in (
                    (even, k, 3 + k, lambda k=k: stills[k, rows]),
                    (odd, 6 + k, 9 + k, lambda k=k: stills[3 + k, rows]),
                    (twice, 12 + k, 12 + k, lambda k=k: 4.0 * shifts[12 + k, y + 8 : y + 8 + CHUNK]),
                ):
                    up, down = shifts[plus, after], shifts[minus, before]
                    both = up + down
                    target[0, k] = still() + both
                    if k < 2:
                        target[1, k] = up - down
                    if k < 1:
                        target[2, k] = both
            total, difference, centre = {}, {}, {}
            for n, key in enumerate(JK):
                ends = even[key] + twice[key]
                under = ring[parity, n, rows]
                over = ends - odd[key]
                total[key] = under + over
                difference[key] = under - over
                centre[key] = middle[n, rows] + total[key]
                ring[parity, n, rows] = ends + odd[key]
                middle[n, rows] = 4.0 * even[key]
            flow = (difference[0, 0], centre[1, 0], centre[0, 1])
            results = (
                centre[0, 0], *flow, total[0, 0], centre[2, 0], centre[0, 2],
                difference[1, 0], difference[0, 1], centre[1, 1],
            )
            for f, value in enumerate(results):
                new[f, z, rows] = value
            for c in range(3):
                start = (c * DEPTH + inner + BZ) * PITCH
                velocity[pl.ds(start + y, CHUNK)] = flow[c]
                if step == 0:
                    velocity[pl.ds(start + SIDE, BXY)] = flow[c]

        @pl.when(z >= 2)
        def _():
            pltpu.make_async_copy(new.at[:, z], out_hbm.at[:, z - 2], out_sem.at[z - 2]).start()

        return carry

    lax.fori_loop(0, PLANES + 2, stream_plane, 0)

    if not last:
        write_plane(sendup_ref, lambda f: new[f, PLANES + 1])
        write_plane(senddown_ref, lambda f: new[f, 2])

    across = functools.partial(
        lax.dot_general, dimension_numbers=(((1,), (1,)), ((), ())), preferred_element_type=F32
    )

    def sample_batch(batch, carry):
        results = []
        for n in range(BATCH):
            above, spots, starts, rows = box_parts(order_ref[batch * BATCH + n])
            cells = jnp.concatenate(
                [
                    jnp.concatenate([velocity[pl.ds(start + i, 8, stride=PITCH)] for i in range(8)], axis=1)
                    for start in starts
                ],
                axis=0,
            )
            results.append((above, rows, across(jnp.concatenate(split(cells), axis=0), spots)))
        for above, rows, found in results:
            plane = lax.broadcasted_iota(jnp.int32, (8, SIDE), 0) + above
            ours = jnp.logical_and(plane >= 0, plane < PLANES)
            for n, start in enumerate(rows):
                value = found[n * 8 : n * 8 + 8] + found[48 + n * 8 : 56 + n * 8]
                sampled[pl.ds(start, 8, stride=BOXED)] = jnp.where(ours, value, 0.0)
        return carry

    lax.fori_loop(0, rounds, sample_batch, 0)

    part_high, part_low = split(
        jnp.concatenate([sampled[chunk_row(n) : chunk_row(n) + ROWS] for n in range(16)], axis=1)
    )
    main = across(jnp.concatenate([part_high, part_low], axis=0), high_ref[...])
    partial = main[:ROWS] + (main[ROWS:] + across(part_high, low_ref[...]))

    newsum_ref[...] = partial if first else sum_ref[...] + partial
    if not last:
        newstate_ref[...] = state[...] + MOBILITY * partial
        for ref, start, owners in ((sendup_ref, GROUP, 3), (senddown_ref, 0, 4)):
            write_tail(
                ref,
                owners,
                lambda owner, part: partial[
                    start + owner * GROUP : start + owner * GROUP + GROUP, part * 128 : part * 128 + 128
                ],
            )
    for z in range(PLANES):
        pltpu.make_async_copy(new.at[:, z + 2], out_hbm.at[:, z], out_sem.at[z]).wait()


def advance(first, last, total_planes, slots, high, low, moments, up, down, *rest):
    square = (SIDE, SIDE)
    out_shape = [
        jax.ShapeDtypeStruct((FIELDS, PLANES) + square, F32),
        jax.ShapeDtypeStruct((ROWS, LANES), F32),
    ]
    out_specs = [HBM, VMEM]
    if not last:
        out_shape += [
            jax.ShapeDtypeStruct((ROWS, LANES), F32),
            jax.ShapeDtypeStruct((message_rows(3), SIDE), F32),
            jax.ShapeDtypeStruct((message_rows(4), SIDE), F32),
        ]
        out_specs += [VMEM] * 3
    if first:
        out_shape.append(jax.ShapeDtypeStruct((ORDER,), jnp.int32))
        out_specs.append(SMEM)
        out_shape.append(jax.ShapeDtypeStruct((1, 128), jnp.int32))
        out_specs.append(VMEM)
    scratch = [
        pltpu.VMEM((FIELDS, PLANES + 2) + square, F32),
        pltpu.VMEM((FIELDS, PLANES + 2) + square, F32),
        pltpu.VMEM((3 * DEPTH * PITCH, SIDE), F32),
        pltpu.VMEM((3 * DEPTH * PITCH, SIDE), F32),
        pltpu.VMEM((CELLS // 128 * BOXED, 128), F32),
        pltpu.VMEM((CELLS // 128 * BOXED, 128), F32),
        pltpu.VMEM((15, PADDED, SIDE), F32),
        pltpu.VMEM((6,) + square, F32),
        pltpu.VMEM((2, 6) + square, F32),
        pltpu.VMEM((6,) + square, F32),
        pltpu.VMEM((ROWS, LANES), F32),
        pltpu.SemaphoreType.DMA((PLANES,)),
        pltpu.SemaphoreType.DMA((PLANES,)),
        pltpu.SemaphoreType.DMA((1,)),
        pltpu.SMEM((1, 128), jnp.int32),
    ]
    return pl.pallas_call(
        functools.partial(step_kernel, first, last, total_planes),
        out_shape=out_shape,
        in_specs=[SMEM, VMEM, VMEM, HBM, VMEM, VMEM] + [VMEM] * 2 + [VMEM if first else SMEM],
        out_specs=out_specs,
        scratch_shapes=scratch,
        compiler_params=pltpu.CompilerParams(vmem_limit_bytes=44 * 2**20),
        cost_estimate=pl.CostEstimate(
            flops=4 * 10**8, bytes_accessed=16 * 2**20, transcendentals=0
        ),
        input_output_aliases={} if first else {3: 0},
        name="first_step" if first else "last_step" if last else "step",
    )(slots, high, low, moments, up, down, *rest)


def per_device(moments, shapes, anchors, synthesis, spreading):
    devices = lax.axis_size("gz")
    total_planes = PLANES * devices
    small, send_up, send_down = pack(moments, jnp.transpose(shapes, (1, 0, 2)), anchors.T)
    up = shifted(send_up, 1)
    down = shifted(send_down, -1)
    below2 = shifted(small, 2)
    above2 = shifted(small, -2)
    high, low = couple(jnp.pad(synthesis, ((0, 0), (0, LANES - COEFS))), spreading)

    slots = jnp.full((1,), PLANES * lax.axis_index("gz"), jnp.int32)

    rest = (small, below2, above2)
    for step in range(STEPS):
        last = step == STEPS - 1
        results = advance(step == 0, last, total_planes, slots, high, low, moments, up, down, *rest)
        moments, sums = results[:2]
        if not last:
            state, send_up, send_down = results[2:5]
            if step == 0:
                order, slots = results[5:]
            up, down = shifted(send_up, 1), shifted(send_down, -1)
            rest = (state, sums, order)

    group = [sums[i * GROUP : (i + 1) * GROUP] for i in range(BLOCKS)]
    change = group[2] + shifted(group[3], 1) + shifted(group[1], -1) + shifted(group[0], -2)
    change = jnp.transpose(change.reshape(3, OWNED, LANES)[:, :, :COEFS], (1, 0, 2))
    return (moments, shapes + MOBILITY * change)


def solution(mesh):
    return jax.shard_map(
        per_device,
        mesh=mesh,
        in_specs=(P(None, "gz", None, None), P("gz", None, None), P("gz", None), P(), P()),
        out_specs=(P(None, "gz", None, None), P("gz", None, None)),
        check_vma=False,
    )
```

```python
import functools

import jax
import jax.numpy as jnp
from jax import lax
from jax.experimental import pallas as pl
from jax.experimental.pallas import tpu as pltpu
from jax.sharding import PartitionSpec as P


LMAX = 16
BZ = 8
BXY = 16
STEPS = 3
STIFF_SCALE = 0.002
MOBILITY = 0.5

PLANES = 8
SIDE = 128
OWNED = 8
COEFS = 289
SLOTS = 40
ORDER = 48
LANES = 384
KEPT = 304
CELLS = 2048
POINTS = 512
GROUP = OWNED * 3
BLOCKS = 5
ROWS = GROUP * BLOCKS
ANCHOR_LANE = 300
FIELDS = 10
SENT = 9 * SIDE
NARROW = COEFS - 256
STEP_LANES = 40
PADDED = 144
PITCH = 145
DEPTH = PLANES + 2 * BZ + 1
BOXED = ROWS + 1
CHUNK = 16
WIDE = 16
UNROLL = 8
BATCH = 4
JK = ((0, 0), (1, 0), (2, 0), (0, 1), (1, 1), (0, 2))

VMEM = pl.BlockSpec(memory_space=pltpu.VMEM)
SMEM = pl.BlockSpec(memory_space=pltpu.SMEM)
HBM = pl.BlockSpec(memory_space=pltpu.HBM)
F32 = jnp.float32
BF16 = jnp.bfloat16


def shifted(block, distance):
    devices = lax.axis_size("gz")
    return lax.ppermute(block, "gz", [((i - distance) % devices, i) for i in range(devices)])


def split(value):
    high = value.astype(BF16)
    return high, (value - high.astype(F32)).astype(BF16)


def tail_rows(owner, part, owners):
    if part < 2:
        group, lane = owner * 2 + part, 0
    else:
        group, lane = owners * 2 + owner // 3, STEP_LANES * (owner % 3)
    start = SENT + group * GROUP
    return slice(start, start + GROUP), lane


def message_rows(owners):
    return SENT + (owners * 2 + (owners + 2) // 3) * GROUP


def read_tail(ref, owner, part, owners):
    rows, lane = tail_rows(owner, part, owners)
    value = ref[rows]
    if part == 2:
        if lane:
            value = pltpu.roll(value, 128 - lane, 1)
        lanes = lax.broadcasted_iota(jnp.int32, value.shape, 1)
        value = jnp.where(lanes < NARROW, value, 0.0)
    return value


def write_tail(ref, values, width):
    owners = values
    for owner in range(owners):
        for part in range(2):
            ref[tail_rows(owner, part, owners)[0]] = width(owner, part)
    for first in range(0, owners, 3):
        packed = width(first, 2)
        for owner in range(first + 1, min(first + 3, owners)):
            packed = packed + pltpu.roll(width(owner, 2), STEP_LANES * (owner - first), 1)
        ref[tail_rows(first, 2, owners)[0]] = packed


def write_plane(ref, field):
    trace = field(4)
    values = [field(0) - 0.6 * trace, field(1), field(2), field(3)]
    values += [field(5) - 0.2 * trace, field(6) - 0.2 * trace, field(7), field(8), field(9)]
    for n, value in enumerate(values):
        ref[n * SIDE : n * SIDE + SIDE] = value


def slot_row(slot):
    return slot + (slot // OWNED) * (2 * OWNED)


def chunk_row(n):
    return (n % 2 * 8 + n // 2) * BOXED


def couple_kernel(synthesis_ref, spreading_ref, high_ref, low_ref):
    width = 512
    turned = jnp.concatenate(split(synthesis_ref[...].T[0:KEPT]), axis=0)
    for ref in (high_ref, low_ref):
        ref[KEPT:] = jnp.zeros((LANES - KEPT, CELLS), BF16)
    for first in range(0, CELLS, width):
        lanes = slice(first, first + width)
        w_high, w_low = split(spreading_ref[:, lanes])
        main = jnp.dot(turned, w_high, preferred_element_type=F32)
        rest = jnp.dot(turned[0:KEPT], w_low, preferred_element_type=F32)
        high_ref[0:KEPT, lanes], low_ref[0:KEPT, lanes] = split(main[:KEPT] + (main[KEPT:] + rest))


def couple(synthesis, spreading):
    shape = jax.ShapeDtypeStruct((LANES, CELLS), BF16)
    return pl.pallas_call(
        couple_kernel,
        out_shape=(shape, shape),
        in_specs=[VMEM, VMEM],
        out_specs=[VMEM, VMEM],
        compiler_params=pltpu.CompilerParams(vmem_limit_bytes=32 * 2**20),
        cost_estimate=pl.CostEstimate(
            flops=6 * LANES * POINTS * CELLS, bytes_accessed=8 * 2**20, transcendentals=0
        ),
        name="couple",
    )(synthesis, spreading)


def pack_kernel(anchors_ref, moments_hbm, shapes_ref, small_ref, up_ref, down_ref, planes, sem):
    copies = [
        pltpu.make_async_copy(moments_hbm.at[:, z], planes.at[n], sem.at[n])
        for n, z in enumerate((PLANES - 1, 0))
    ]
    for copy in copies:
        copy.start()
    small_ref[...] = jnp.zeros_like(small_ref)
    for c in range(3):
        small_ref[c * OWNED : c * OWNED + OWNED, 0:COEFS] = shapes_ref[c]
    part = small_ref[:, 256:LANES]
    row = lax.broadcasted_iota(jnp.int32, part.shape, 0)
    anchor = jnp.zeros(part.shape, jnp.int32)
    for n in range(GROUP):
        anchor = jnp.where(row == n, anchors_ref[n // OWNED, n % OWNED], anchor)
    lane = lax.broadcasted_iota(jnp.int32, part.shape, 1)
    part = jnp.where(lane == ANCHOR_LANE - 256, anchor.astype(F32), part)
    small_ref[:, 256:LANES] = part
    for ref in (up_ref, down_ref):
        write_tail(ref, 1, lambda owner, p: small_ref[:, p * 128 : p * 128 + 128])
    for n, ref in enumerate((up_ref, down_ref)):
        copies[n].wait()
        write_plane(ref, lambda f, n=n: planes[n, f])


def pack(moments, shapes, anchors):
    shape = jax.ShapeDtypeStruct((message_rows(1), SIDE), F32)
    return pl.pallas_call(
        pack_kernel,
        out_shape=(jax.ShapeDtypeStruct((GROUP, LANES), F32), shape, shape),
        in_specs=[SMEM, HBM, VMEM],
        out_specs=[VMEM, VMEM, VMEM],
        scratch_shapes=[pltpu.VMEM((2, FIELDS, SIDE, SIDE), F32), pltpu.SemaphoreType.DMA((2,))],
        compiler_params=pltpu.CompilerParams(vmem_limit_bytes=60 * 2**20),
        name="pack",
    )(anchors, moments, shapes)


def spread_x(zero, one, two):
    plus = zero if two is None else zero + two
    minus = plus
    if one is not None:
        plus, minus = plus + one, plus - one
    plus = pltpu.roll(plus, 1, 1)
    minus = pltpu.roll(minus, SIDE - 1, 1)
    both = plus + minus
    return (4.0 * zero + both, plus - minus, both)


def collide_rows(m, force):
    unit = 1.0 / 216.0
    rho = m[0]
    u = [m[1 + a] + 0.5 * force[a] for a in range(3)]
    t = [0.625 * u[a] + 0.375 * force[a] for a in range(3)]
    v = [(9.0 * unit) * u[a] for a in range(3)]
    line = [(3.0 * unit) * (m[1 + a] + force[a]) for a in range(3)]
    shared = (0.375 * unit) * rho
    square = [shared - (1.125 * unit) * m[4 + a] + v[a] * t[a] for a in range(3)]
    cross = [
        v[a] * t[b] + v[b] * t[a] - (2.25 * unit) * m[7 + n]
        for n, (a, b) in enumerate(((0, 1), (0, 2), (1, 2)))
    ]
    cell = unit * rho - (1.0 / 3.0) * (square[0] + square[1] + square[2])
    return cell, line, square, cross


def step_kernel(first, last, total_planes, *refs):
    refs = list(refs)

    def take(count):
        taken = refs[:count]
        del refs[:count]
        return taken

    slots_ref, high_ref, low_ref, moments_hbm, up_ref, down_ref = take(6)
    if first:
        own_ref, below_ref, above_ref = take(3)
    else:
        state_ref, sum_ref, order_ref = take(3)
    out_hbm, newsum_ref = take(2)
    if not last:
        newstate_ref, sendup_ref, senddown_ref = take(3)
    if first:
        order_ref, places_ref = take(2)
    (
        old, new, velocity, force, boxes, sampled,
        shifts, stills, ring, middle, state,
        in_sem, out_sem, slot_sem, slots_smem,
    ) = refs

    for z in range(PLANES):
        pltpu.make_async_copy(moments_hbm.at[:, z], old.at[:, z + 1], in_sem.at[z]).start()

    if first:
        home_ref, slots_ref = slots_ref, slots_smem
        row = lax.broadcasted_iota(jnp.int32, (GROUP, 128), 0)
        lane = lax.broadcasted_iota(jnp.int32, (GROUP, 128), 1)
        last_part = tail_rows(0, 2, 1)[0]
        values = (
            below_ref[:, 256:LANES], up_ref[last_part], own_ref[:, 256:LANES],
            down_ref[last_part], above_ref[:, 256:LANES],
        )
        edge = ANCHOR_LANE - 256
        spots = jnp.zeros((GROUP, 128), F32)
        for owner, value in enumerate(values):
            column = jnp.broadcast_to(value[:, edge : edge + 1], (GROUP, 128))
            spots = jnp.where(lane == row + owner * GROUP, column, spots)
        spots = jnp.sum(spots, axis=0, keepdims=True).astype(jnp.int32)
        lane = lane[0:1]
        along = functools.reduce(
            jnp.logical_or,
            [
                jnp.logical_and(lane >= owner * GROUP, lane < owner * GROUP + OWNED)
                for owner in range(BLOCKS)
            ],
        )
        half = total_planes // 2
        local = ((spots - home_ref[0] + half) & (total_planes - 1)) - half
        places_ref[...] = jnp.where(along, local, spots)
        copy = pltpu.make_async_copy(places_ref, slots_smem, slot_sem.at[0])
        copy.start()
        copy.wait()

    if first:

        def scan(slot, carry):
            count, spare = carry
            above = slots_ref[0, slot_row(slot)]
            near = jnp.logical_and(above >= -BZ, above <= PLANES)

            order_ref[count] = slot
            return count + near.astype(jnp.int32), jnp.where(near, spare, slot)

        count, spare = lax.fori_loop(0, SLOTS, scan, (jnp.int32(0), jnp.int32(0)), unroll=8)
        for n in range(BATCH - 1):
            order_ref[count + n] = spare
        order_ref[ORDER - 1] = (count + BATCH - 1) // BATCH
    rounds = order_ref[ORDER - 1]

    for c in range(3):
        start = (c * DEPTH + BZ - 1) * PITCH
        force[start : start + (PLANES + 2) * PITCH] = jnp.zeros(((PLANES + 2) * PITCH, SIDE), F32)
    sampled[...] = jnp.zeros_like(sampled)
    for ref, edge in ((up_ref, 0), (down_ref, PLANES + 1)):
        for n, f in enumerate((0, 1, 2, 3, 5, 6, 7, 8, 9)):
            old[f, edge] = ref[n * SIDE : n * SIDE + SIDE]
        old[4, edge] = jnp.zeros((SIDE, SIDE), F32)

    for part in range(3):
        lanes = slice(part * 128, part * 128 + 128)
        for owner in range(BLOCKS):
            rows = slice(owner * GROUP, owner * GROUP + GROUP)
            if first:
                if owner % 2 == 1:
                    value = read_tail(up_ref if owner == 1 else down_ref, 0, part, 1)
                else:
                    value = (below_ref, own_ref, above_ref)[owner // 2][:, lanes]
                    if part == 2:
                        lane = lax.broadcasted_iota(jnp.int32, value.shape, 1)
                        value = jnp.where(lane < NARROW, value, 0.0)
            else:
                value = state_ref[rows, lanes]
                if owner < 3:
                    value = value + MOBILITY * read_tail(up_ref, owner, part, 3)
                if owner > 0:
                    value = value + MOBILITY * read_tail(down_ref, owner - 1, part, 4)
            state[rows, lanes] = value

    number = lax.broadcasted_iota(jnp.int32, (1, LANES), 1)
    degree = jnp.zeros((1, LANES), jnp.int32)
    for step in range(1, LMAX + 1):
        degree = degree + (number >= step * step).astype(jnp.int32)
    stiffness = STIFF_SCALE * (degree * (degree + 1) + 2).astype(F32)
    coef_high, coef_low = split(-stiffness * state[...])
    both = jnp.concatenate([coef_high, coef_low], axis=0)
    for part in range(CELLS // 512):
        lanes = slice(part * 512, part * 512 + 512)
        main = jnp.dot(both, high_ref[:, lanes], preferred_element_type=F32)
        rest = jnp.dot(coef_high, low_ref[:, lanes], preferred_element_type=F32)
        whole = main[:ROWS] + (main[ROWS:] + rest)
        for chunk in range(4):
            start = chunk_row(part * 4 + chunk)
            boxes[start : start + ROWS] = whole[:, chunk * 128 : chunk * 128 + 128]

    def box_parts(slot):
        base = slot_row(slot)
        above = slots_ref[0, base]
        near = jnp.logical_and(above >= -BZ, above <= PLANES)
        above = jnp.where(near, above, PLANES + 1)
        row = slots_ref[0, base + OWNED]
        column = slots_ref[0, base + 2 * OWNED]
        lane = lax.broadcasted_iota(jnp.int32, (BXY, SIDE), 1)
        inside = lax.broadcasted_iota(jnp.int32, (BXY, SIDE), 0)
        hit = (((lane - column) & (SIDE - 1)) == inside).astype(F32).astype(BF16)
        none = jnp.zeros((BXY, SIDE), BF16)
        spots = jnp.concatenate(
            [jnp.concatenate([hit if i == n else none for i in range(8)], axis=1) for n in range(8)],
            axis=0,
        )
        starts = [
            (c * DEPTH + above + BZ) * PITCH + row + half * 8 for c in range(3) for half in range(2)
        ]
        rows = [half * 8 * BOXED + base + c * OWNED for c in range(3) for half in range(2)]
        return above, spots, starts, rows

    def place_batch(batch, carry):
        found = []
        for n in range(BATCH):
            _, spots, starts, rows = box_parts(order_ref[batch * BATCH + n])
            cells = jnp.concatenate([boxes[pl.ds(start, 8, stride=BOXED)] for start in rows], axis=0)
            placed = jnp.dot(
                jnp.concatenate(split(cells), axis=1),
                jnp.concatenate([spots, spots], axis=0),
                preferred_element_type=F32,
            )
            found.append((starts, placed))
        for starts, placed in found:
            where = [
                (pl.ds(start + i, 8, stride=PITCH), slice(n * 8, n * 8 + 8), slice(i * 128, i * 128 + 128))
                for n, start in enumerate(starts)
                for i in range(8)
            ]
            sums = [force[there] + placed[here, lanes] for there, here, lanes in where]
            for (there, here, lanes), value in zip(where, sums):
                force[there] = value
        return carry

    lax.fori_loop(0, rounds, place_batch, 0)

    def fold(z, carry):
        for c in range(3):
            start = (c * DEPTH + z + BZ - 1) * PITCH
            first = pl.ds(start, BXY)
            force[first] = force[first] + force[pl.ds(start + SIDE, BXY)]
        return carry

    lax.fori_loop(0, PLANES + 2, fold, 0)

    def stream_edge(z, sign):
        add = jnp.add if sign > 0 else jnp.subtract
        for step in range(SIDE // WIDE):
            y = step * WIDE
            rows = slice(y, y + WIDE)
            m = [old[f, z, rows] for f in range(FIELDS)]
            starts = [(c * DEPTH + z + BZ - 1) * PITCH + y for c in range(3)]
            cell, line, square, cross = collide_rows(m, [force[n : n + WIDE] for n in starts])
            even = [
                spread_x(add(cell + square[0], line[0]), add(line[2], cross[1]), square[2]),
                spread_x(add(line[1], cross[0]), cross[2], None),
                spread_x(square[1], None, None),
            ]
            moved = slice(y + 8, y + 8 + WIDE)
            for k in range(3):
                ends = even[0][k] + even[2][k]
                shifts[k, moved] = ends + even[1][k]
                shifts[3 + k, moved] = ends - even[1][k]
                stills[k, rows] = 4.0 * even[0][k]
        for field in range(6):
            shifts[field, 7:8] = shifts[field, SIDE + 7 : SIDE + 8]
            shifts[field, SIDE + 8 : SIDE + 9] = shifts[field, 8:9]
        for step in range(SIDE // CHUNK):
            y = step * CHUNK
            rows = slice(y, y + CHUNK)
            even = {}
            for k in range(3):
                up, down = shifts[k, y + 7 : y + 7 + CHUNK], shifts[3 + k, y + 9 : y + 9 + CHUNK]
                both = up + down
                even[0, k] = stills[k, rows] + both
                even[1, k] = up - down
                even[2, k] = both
            if sign > 0:
                for n, key in enumerate(JK):
                    ring[z % 2, n, rows] = even[key]
            else:
                finish(z, z % 2, PLANES - 1, y, {key: even[key] for key in JK})

    def finish(z, parity, inner, y, over):
        rows = slice(y, y + CHUNK)
        total, difference, centre = {}, {}, {}
        for n, key in enumerate(JK):
            under = ring[parity, n, rows]
            total[key] = under + over[key]
            difference[key] = under - over[key]
            centre[key] = middle[n, rows] + total[key]
        flow = (difference[0, 0], centre[1, 0], centre[0, 1])
        results = (
            centre[0, 0], *flow, total[0, 0], centre[2, 0], centre[0, 2],
            difference[1, 0], difference[0, 1], centre[1, 1],
        )
        for f, value in enumerate(results):
            new[f, z, rows] = value
        for c in range(3):
            start = (c * DEPTH + inner + BZ) * PITCH
            velocity[pl.ds(start + y, CHUNK)] = flow[c]
            if y == 0:
                velocity[pl.ds(start + SIDE, BXY)] = flow[c]

    def stream_plane(z, carry):
        pltpu.make_async_copy(moments_hbm.at[:, 0], old.at[:, z], in_sem.at[z - 1]).wait()


        def collide_chunk(y):
            rows = pl.ds(y, WIDE)
            m = [old[f, z, rows] for f in range(FIELDS)]
            cell, line, square, cross = collide_rows(
                m, [force[pl.ds((c * DEPTH + z + BZ - 1) * PITCH + y, WIDE)] for c in range(3)]
            )
            even = [
                spread_x(cell, line[2], square[2]),
                spread_x(line[1], cross[2], None),
                spread_x(square[1], None, None),
            ]
            twice = spread_x(square[0], None, None)
            odd = [spread_x(line[0], cross[1], None), spread_x(cross[0], None, None)]
            moved = pl.ds(y + 8, WIDE)
            for k in range(3):
                ends = even[0][k] + even[2][k]
                shifts[k, moved] = ends + even[1][k]
                shifts[3 + k, moved] = ends - even[1][k]
                shifts[6 + k, moved] = odd[0][k] + odd[1][k]
                shifts[9 + k, moved] = odd[0][k] - odd[1][k]
                shifts[12 + k, moved] = twice[k]
                stills[k, rows] = 4.0 * even[0][k]
                stills[3 + k, rows] = 4.0 * odd[0][k]

        def collide_some(step, carry):
            for n in range(UNROLL):
                collide_chunk(pl.multiple_of(step * (WIDE * UNROLL), WIDE * UNROLL) + n * WIDE)
            return carry

        lax.fori_loop(0, SIDE // (WIDE * UNROLL), collide_some, 0)
        for field in range(15):
            shifts[field, 7:8] = shifts[field, SIDE + 7 : SIDE + 8]
            shifts[field, SIDE + 8 : SIDE + 9] = shifts[field, 8:9]
        parity = z % 2
        inner = jnp.clip(z - 2, 0, PLANES - 1)

        for step in range(SIDE // CHUNK):
            y = step * CHUNK
            rows = slice(y, y + CHUNK)
            after = slice(y + 7, y + 7 + CHUNK)
            before = slice(y + 9, y + 9 + CHUNK)
            even, odd, twice = {}, {}, {}
            for k in range(3):
                for target, plus, minus, still in (
                    (even, k, 3 + k, lambda k=k: stills[k, rows]),
                    (odd, 6 + k, 9 + k, lambda k=k: stills[3 + k, rows]),
                    (twice, 12 + k, 12 + k, lambda k=k: 4.0 * shifts[12 + k, y + 8 : y + 8 + CHUNK]),
                ):
                    up, down = shifts[plus, after], shifts[minus, before]
                    both = up + down
                    target[0, k] = still() + both
                    if k < 2:
                        target[1, k] = up - down
                    if k < 1:
                        target[2, k] = both
            ends = {key: even[key] + twice[key] for key in JK}
            finish(z, parity, inner, y, {key: ends[key] - odd[key] for key in JK})
            for n, key in enumerate(JK):
                ring[parity, n, rows] = ends[key] + odd[key]
                middle[n, rows] = 4.0 * even[key]

        @pl.when(z >= 2)
        def _():
            pltpu.make_async_copy(new.at[:, z], out_hbm.at[:, z - 2], out_sem.at[z - 2]).start()

        return carry

    stream_edge(0, 1)
    lax.fori_loop(1, PLANES + 1, stream_plane, 0)
    stream_edge(PLANES + 1, -1)
    pltpu.make_async_copy(new.at[:, PLANES + 1], out_hbm.at[:, PLANES - 1], out_sem.at[PLANES - 1]).start()

    if not last:
        write_plane(sendup_ref, lambda f: new[f, PLANES + 1])
        write_plane(senddown_ref, lambda f: new[f, 2])

    across = functools.partial(
        lax.dot_general, dimension_numbers=(((1,), (1,)), ((), ())), preferred_element_type=F32
    )

    def sample_batch(batch, carry):
        results = []
        for n in range(BATCH):
            above, spots, starts, rows = box_parts(order_ref[batch * BATCH + n])
            cells = jnp.concatenate(
                [
                    jnp.concatenate([velocity[pl.ds(start + i, 8, stride=PITCH)] for i in range(8)], axis=1)
                    for start in starts
                ],
                axis=0,
            )
            results.append((above, rows, across(jnp.concatenate(split(cells), axis=0), spots)))
        for above, rows, found in results:
            plane = lax.broadcasted_iota(jnp.int32, (8, SIDE), 0) + above
            ours = jnp.logical_and(plane >= 0, plane < PLANES)
            for n, start in enumerate(rows):
                value = found[n * 8 : n * 8 + 8] + found[48 + n * 8 : 56 + n * 8]
                sampled[pl.ds(start, 8, stride=BOXED)] = jnp.where(ours, value, 0.0)
        return carry

    lax.fori_loop(0, rounds, sample_batch, 0)

    part_high, part_low = split(
        jnp.concatenate([sampled[chunk_row(n) : chunk_row(n) + ROWS] for n in range(16)], axis=1)
    )
    main = across(jnp.concatenate([part_high, part_low], axis=0), high_ref[...])
    partial = main[:ROWS] + (main[ROWS:] + across(part_high, low_ref[...]))

    newsum_ref[...] = partial if first else sum_ref[...] + partial
    if not last:
        newstate_ref[...] = state[...] + MOBILITY * partial
        for ref, start, owners in ((sendup_ref, GROUP, 3), (senddown_ref, 0, 4)):
            write_tail(
                ref,
                owners,
                lambda owner, part: partial[
                    start + owner * GROUP : start + owner * GROUP + GROUP, part * 128 : part * 128 + 128
                ],
            )
    for z in range(PLANES):
        pltpu.make_async_copy(new.at[:, z + 2], out_hbm.at[:, z], out_sem.at[z]).wait()


def advance(first, last, total_planes, slots, high, low, moments, up, down, *rest):
    square = (SIDE, SIDE)
    out_shape = [
        jax.ShapeDtypeStruct((FIELDS, PLANES) + square, F32),
        jax.ShapeDtypeStruct((ROWS, LANES), F32),
    ]
    out_specs = [HBM, VMEM]
    if not last:
        out_shape += [
            jax.ShapeDtypeStruct((ROWS, LANES), F32),
            jax.ShapeDtypeStruct((message_rows(3), SIDE), F32),
            jax.ShapeDtypeStruct((message_rows(4), SIDE), F32),
        ]
        out_specs += [VMEM] * 3
    if first:
        out_shape.append(jax.ShapeDtypeStruct((ORDER,), jnp.int32))
        out_specs.append(SMEM)
        out_shape.append(jax.ShapeDtypeStruct((1, 128), jnp.int32))
        out_specs.append(VMEM)
    scratch = [
        pltpu.VMEM((FIELDS, PLANES + 2) + square, F32),
        pltpu.VMEM((FIELDS, PLANES + 2) + square, F32),
        pltpu.VMEM((3 * DEPTH * PITCH, SIDE), F32),
        pltpu.VMEM((3 * DEPTH * PITCH, SIDE), F32),
        pltpu.VMEM((CELLS // 128 * BOXED, 128), F32),
        pltpu.VMEM((CELLS // 128 * BOXED, 128), F32),
        pltpu.VMEM((15, PADDED, SIDE), F32),
        pltpu.VMEM((6,) + square, F32),
        pltpu.VMEM((2, 6) + square, F32),
        pltpu.VMEM((6,) + square, F32),
        pltpu.VMEM((ROWS, LANES), F32),
        pltpu.SemaphoreType.DMA((PLANES,)),
        pltpu.SemaphoreType.DMA((PLANES,)),
        pltpu.SemaphoreType.DMA((1,)),
        pltpu.SMEM((1, 128), jnp.int32),
    ]
    return pl.pallas_call(
        functools.partial(step_kernel, first, last, total_planes),
        out_shape=out_shape,
        in_specs=[SMEM, VMEM, VMEM, HBM, VMEM, VMEM] + [VMEM] * 2 + [VMEM if first else SMEM],
        out_specs=out_specs,
        scratch_shapes=scratch,
        compiler_params=pltpu.CompilerParams(vmem_limit_bytes=44 * 2**20),
        cost_estimate=pl.CostEstimate(
            flops=4 * 10**8, bytes_accessed=16 * 2**20, transcendentals=0
        ),
        input_output_aliases={} if first else {3: 0},
        name="first_step" if first else "last_step" if last else "step",
    )(slots, high, low, moments, up, down, *rest)


def per_device(moments, shapes, anchors, synthesis, spreading):
    devices = lax.axis_size("gz")
    total_planes = PLANES * devices
    small, send_up, send_down = pack(moments, jnp.transpose(shapes, (1, 0, 2)), anchors.T)
    up = shifted(send_up, 1)
    down = shifted(send_down, -1)
    below2 = shifted(small, 2)
    above2 = shifted(small, -2)
    high, low = couple(jnp.pad(synthesis, ((0, 0), (0, LANES - COEFS))), spreading)

    slots = jnp.full((1,), PLANES * lax.axis_index("gz"), jnp.int32)

    rest = (small, below2, above2)
    for step in range(STEPS):
        last = step == STEPS - 1
        results = advance(step == 0, last, total_planes, slots, high, low, moments, up, down, *rest)
        moments, sums = results[:2]
        if not last:
            state, send_up, send_down = results[2:5]
            if step == 0:
                order, slots = results[5:]
            up, down = shifted(send_up, 1), shifted(send_down, -1)
            rest = (state, sums, order)

    group = [sums[i * GROUP : (i + 1) * GROUP] for i in range(BLOCKS)]
    change = group[2] + shifted(group[3], 1) + shifted(group[1], -1) + shifted(group[0], -2)
    change = jnp.transpose(change.reshape(3, OWNED, LANES)[:, :, :COEFS], (1, 0, 2))
    return (moments, shapes + MOBILITY * change)


def solution(mesh):
    return jax.shard_map(
        per_device,
        mesh=mesh,
        in_specs=(P(None, "gz", None, None), P("gz", None, None), P("gz", None), P(), P()),
        out_specs=(P(None, "gz", None, None), P("gz", None, None)),
        check_vma=False,
    )
```
